32 devices in a mesh: row: 8 (over y, x, core), col: 4 (over z).
Axes of the slice: x: 2, y: 2, z: 4, core: 2. Of those that a mesh axis runs over, the one named last changes fastest.
Arguments:
- tokens: bfloat16 [4, 4096, 1792], P(None, ('row', 'col')), may hold values from -12 to 12
- lengths: int32 [4, 8], replicated, may hold values from 1 to 1024, 4096 in all within a row
- permutation: int32 [4, 32], replicated, may hold values from 0 to 31, each once within a row
- cotangent: bfloat16 [4, 4096, 1792], P(None, ('row', 'col')), may hold values from -12 to 12
- norm1_gain: float32 [1792], replicated, may hold values from 0.5 to 1.5
- mixer_in: bfloat16 [1792, 1792], P('row', 'col'), may hold values from -0.125 to 0.125
- mixer_gate: bfloat16 [1792, 1792], P('row', 'col'), may hold values from -0.125 to 0.125
- conv_kernel: float32 [3, 1792], P(None, 'col'), may hold values from -2.5 to 2.5
- mixer_out: bfloat16 [1792, 1792], P('row', 'col'), may hold values from -0.125 to 0.125
- norm2_gain: float32 [1792], replicated, may hold values from 0.5 to 1.5
- ffn_gate: bfloat16 [1792, 4864], P('row', 'col'), may hold values from -0.125 to 0.125
- ffn_up: bfloat16 [1792, 4864], P('row', 'col'), may hold values from -0.125 to 0.125
- ffn_down: bfloat16 [1792, 4864], P('row', 'col'), may hold values from -0.078125 to 0.078125
Outputs:
- output: bfloat16 [4, 4096, 1792], P(None, ('row', 'col'))
- input_grad: float32 [4, 4096, 1792], P(None, ('row', 'col'))
- norm1_gain_grad: float32 [1792], P(('row', 'col'))
- mixer_in_grad: float32 [1792, 1792], P('row', 'col')
- mixer_gate_grad: float32 [1792, 1792], P('row', 'col')
- conv_kernel_grad: float32 [3, 1792], P(None, ('col', 'row'))
- mixer_out_grad: float32 [1792, 1792], P('row', 'col')
- norm2_gain_grad: float32 [1792], P(('row', 'col'))
- ffn_gate_grad: float32 [1792, 4864], P('row', 'col')
- ffn_up_grad: float32 [1792, 4864], P('row', 'col')
- ffn_down_grad: float32 [1792, 4864], P('row', 'col')
The draws below stay inside these ranges and needn't reach their ends.
Inputs may be any that keep to these rules, and one draw needn't show every extreme that they name: Each row of lengths sums to 4096, and its largest entry is exactly 1024. `permutation`: each row holds every number of 0 to 31 once.
All inputs are finite; a program needn't handle non-finite values.
Results may differ from the reference program's by a relative error of at most 0.0083.
Values may be sent and summed in bfloat16 or wider, within the bound.
No kernel may reach another device: no remote copies, remote signals or barrier semaphores. Data moves between devices by JAX's collectives and lax.ppermute only.
A program may use at most 160 MiB of HBM per device.

```python
import math
from functools import partial
import jax
import jax.numpy as jnp
import numpy as np
from jax import lax

D = 1792
FF = 4864
MB = 4
BLOCK = 128
MAXLEN = 1024
TMB = 4096
NB = 32
SEQS = 8


def feature_field(key):
    full_shape = (MB, TMB, D)
    column = jnp.arange(D, dtype=jnp.float32) / D
    first_key, second_key = jax.random.split(key)
    values = jnp.clip(jax.random.normal(first_key, full_shape, jnp.float32), -4.0, 4.0)
    row_scale = jnp.exp(jax.random.uniform(second_key, (MB, TMB, 1), jnp.float32, -0.5, 0.5))
    return values * row_scale * 3.0 ** (column - 0.5)


def draw_tokens(key, part):
    return feature_field(jax.random.fold_in(key, 11)).astype(jnp.bfloat16)


def draw_cotangent(key, part):
    return feature_field(jax.random.fold_in(key, 23)).astype(jnp.bfloat16)


def block_levels(rng, shape, cuts, low, top_value):
    loudness, own = 1.0, jax.random.fold_in(rng, 6)
    for dim, shards_of in cuts:
        steps = jnp.exp(jax.random.uniform(jax.random.fold_in(own, dim), (shards_of,), jnp.float32, low / len(cuts), top_value / len(cuts)))
        loudness = loudness * jnp.repeat(steps, shape[dim] // shards_of).reshape([-1 if axis == dim else 1 for axis in range(len(shape))])
    return loudness


def length_profile(count, total, limit, skew):
    weights = [(1 << 20) // math.isqrt(rank ** skew) + 1 for rank in range(2, count + 1)]
    rest, holding = total - limit - (count - 1), [1] * (count - 1)
    while rest > 0:
        free = [i for i in range(count - 1) if holding[i] < limit]
        pool, budget = sum([weights[i] for i in free]), rest
        for i in free:
            addition = min(limit - holding[i], max(1, budget * weights[i] // pool), rest)
            holding[i] = holding[i] + addition
            rest = rest - addition
    return np.array([limit] + holding)


def ragged(own_key, amount, total, reach, skew):
    if amount == 2:
        one = jax.random.randint(own_key, (), max(1, total - reach), min(reach, total - 1) + 1)
        return jnp.stack([one, total - one])
    tallies = jnp.asarray(length_profile(amount, total, reach, skew), jnp.int32)
    couples = (amount - 1) // 2
    giver, receiver = tallies[1:1 + 2 * couples:2], tallies[2:2 + 2 * couples:2]
    room = jnp.minimum(giver - 1, reach - receiver)
    passed = jax.random.randint(jax.random.fold_in(own_key, 1), (couples,), 0, 1 << 20) % (room + 1)
    tallies = tallies.at[1:1 + 2 * couples:2].set(giver - passed).at[2:2 + 2 * couples:2].set(receiver + passed)
    return tallies[jax.random.permutation(jax.random.fold_in(own_key, 2), amount)]


def centred(stream_key, dims, scale, limit, cuts=(), kind=jnp.bfloat16):
    gain = block_levels(stream_key, dims, cuts, -0.22, 0.18) if cuts else 1.0
    entries = jax.random.normal(stream_key, dims, jnp.float32) * scale * gain
    return jnp.minimum(jnp.maximum(entries, -limit), limit).astype(kind)


def setup_inputs(seed: int = 0) -> dict:
    streams_of = jax.random.split(jax.random.key(seed), 14)
    return {
        "tokens": draw_tokens(jax.random.fold_in(streams_of[13], 71), 0),
        "lengths": jax.vmap(lambda own: ragged(own, SEQS, TMB, MAXLEN, 1))(jax.random.split(streams_of[1], MB)).reshape((MB, SEQS)).astype(jnp.int32),
        "permutation": jax.vmap(lambda own: jax.random.permutation(own, NB))(jax.random.split(streams_of[2], MB)).reshape((MB, NB)).astype(jnp.int32),
        "cotangent": draw_cotangent(jax.random.fold_in(streams_of[13], 71), 0),
        "norm1_gain": jnp.clip(1.0 + 0.1 * jax.random.normal(streams_of[4], (D,), jnp.float32), 0.5, 1.5),
        "mixer_in": centred(streams_of[5], (D, D), D ** -0.5, 0.125, ((0, 8), (1, 4))),
        "mixer_gate": centred(streams_of[6], (D, D), D ** -0.5, 0.125, ((0, 8), (1, 4))),
        "conv_kernel": centred(streams_of[7], (3, D), 0.6, 2.5, ((1, 4),), jnp.float32),
        "mixer_out": centred(streams_of[8], (D, D), D ** -0.5, 0.125, ((0, 8), (1, 4))),
        "norm2_gain": jnp.clip(1.0 + 0.1 * jax.random.normal(streams_of[9], (D,), jnp.float32), 0.5, 1.5),
        "ffn_gate": centred(streams_of[10], (D, FF), D ** -0.5, 0.125, ((0, 8), (1, 4))),
        "ffn_up": centred(streams_of[11], (D, FF), D ** -0.5, 0.125, ((0, 8), (1, 4))),
        "ffn_down": centred(streams_of[12], (D, FF), FF ** -0.5, 0.078125, ((0, 8), (1, 4))),
    }


@jax.custom_vjp
def low(v):
    return lax.optimization_barrier(v.astype(jnp.bfloat16)).astype(jnp.float32)

@jax.custom_vjp
def low_back(v):
    return v

def low_keep(v):
    return (low(v), None)

def low_pass(kept, grad):
    return (grad,)

def back_keep(v):
    return (v, None)

def back_low(kept, grad):
    return (low(grad),)
low.defvjp(low_keep, low_pass)
low_back.defvjp(back_keep, back_low)
EPSILON = 1e-05

def matmul(left, right):
    return jnp.dot(left, right, precision=lax.Precision.HIGHEST, preferred_element_type=jnp.float32)

def rms_scale(values):
    return values * lax.rsqrt(lax.optimization_barrier(jnp.mean(values * values, axis=-1, keepdims=True)) + EPSILON)

def block_layer(params, block_in, keep_one, keep_two):
    gain_one, w_in, w_gate, kernel, w_out, gain_two, w_ffg, w_ffu, w_down = params
    hidden_one = low(rms_scale(block_in) * gain_one)
    signal = low_back(matmul(hidden_one, w_in))
    gating = low_back(matmul(hidden_one, w_gate))
    zero_row = jnp.zeros((1, signal.shape[1]), jnp.float32)
    back_one = jnp.concatenate([zero_row, signal[:-1]], axis=0)
    back_two = jnp.concatenate([zero_row, zero_row, signal[:-2]], axis=0)
    mixed_sig = kernel[0] * signal + kernel[1] * (keep_one * back_one) + kernel[2] * (keep_two * back_two)
    product = low(mixed_sig * gating)
    residual = block_in + low_back(matmul(product, w_out.T))
    hidden_two = low(rms_scale(residual) * gain_two)
    gate_val = low_back(matmul(hidden_two, w_ffg))
    up_val = low_back(matmul(hidden_two, w_ffu))
    activated = low(jax.nn.silu(gate_val) * up_val)
    return residual + low_back(matmul(activated, w_down.T))

def masks_for(seq_len, count):
    offsets = jnp.cumsum(seq_len) - seq_len
    position = jnp.arange(count, dtype=jnp.int32)
    is_start = jnp.any(position[:, None] == offsets[None, :], axis=1)
    was_start = jnp.concatenate([jnp.ones((1,), bool), is_start[:-1]])
    keep_one = jnp.where(is_start, 0.0, 1.0).astype(jnp.float32)[:, None]
    keep_two = jnp.where(is_start | was_start, 0.0, 1.0).astype(jnp.float32)[:, None]
    return (keep_one, keep_two)

def to_initial(values, dealt_order):
    blocks = values.reshape(dealt_order.shape[0], BLOCK, values.shape[1])
    inverse = jnp.zeros_like(dealt_order).at[dealt_order].set(jnp.arange(dealt_order.shape[0], dtype=jnp.int32))
    return jnp.take(blocks, inverse, axis=0).reshape(values.shape)

def to_dealt(values, dealt_order):
    blocks = values.reshape(dealt_order.shape[0], BLOCK, values.shape[1])
    return jnp.take(blocks, dealt_order, axis=0).reshape(values.shape)

def reference(tokens, lengths, permutation, cotangent, norm1_gain, mixer_in, mixer_gate, conv_kernel, mixer_out, norm2_gain, ffn_gate, ffn_up, ffn_down):
    initials = jax.vmap(to_initial)(tokens.astype(jnp.float32), permutation)
    cot_orig = jax.vmap(to_initial)(cotangent.astype(jnp.float32), permutation)
    keep_one, keep_two = jax.vmap(partial(masks_for, count=TMB))(lengths)
    params = (norm1_gain, mixer_in.astype(jnp.float32), mixer_gate.astype(jnp.float32), conv_kernel, mixer_out.astype(jnp.float32), norm2_gain, ffn_gate.astype(jnp.float32), ffn_up.astype(jnp.float32), ffn_down.astype(jnp.float32))

    def whole_pass(params, inputs):

        def single_micro(pieces):
            return jax.checkpoint(block_layer)(params, pieces[0], pieces[1], pieces[2])
        return lax.map(single_micro, (inputs, keep_one, keep_two))
    result, pull_back = jax.vjp(whole_pass, params, initials)
    grad_params, grad_inputs = pull_back(cot_orig)
    output = jax.vmap(to_dealt)(result, permutation).astype(jnp.bfloat16)
    input_grad = jax.vmap(to_dealt)(grad_inputs, permutation)
    return (output, input_grad, grad_params[0], grad_params[1], grad_params[2], grad_params[3], grad_params[4], grad_params[5], grad_params[6], grad_params[7], grad_params[8])
```

```python
import jax
import jax.numpy as jnp
from jax import lax
from jax.sharding import Mesh
from jax.sharding import PartitionSpec as P

BLOCK = 128
EPSILON = 1e-05
F32 = jnp.float32
BF16 = jnp.bfloat16
EVERY = ("a", "b", "c", "z")


def dot_nn(left, right):
    return lax.dot_general(left, right, (((1,), (0,)), ((), ())), preferred_element_type=F32)


def dot_nt(left, right):
    return lax.dot_general(left, right, (((1,), (1,)), ((), ())), preferred_element_type=F32)


def dot_tn(left, right):
    return lax.dot_general(left, right, (((0,), (0,)), ((), ())), preferred_element_type=F32)


def shift_by(value, axis, amount):
    size = lax.axis_size(axis)
    return lax.ppermute(value, axis, [(i, (i + amount) % size) for i in range(size)])


def pieces_of(value, axis):
    return [value] + [shift_by(value, axis, s) for s in range(1, lax.axis_size(axis))]


def in_order(pieces, axis, dim):
    size, index = len(pieces), lax.axis_index(axis)
    if size == 2:
        first = index == 0
        return jnp.stack(
            [jnp.where(first, pieces[0], pieces[1]), jnp.where(first, pieces[1], pieces[0])], axis=dim
        )
    return jnp.stack(
        [lax.select_n((index - j) % size, *pieces) for j in range(size)], axis=dim
    )


def scatter_sum(value, axis, dim):
    size, index = lax.axis_size(axis), lax.axis_index(axis)
    total = lax.dynamic_index_in_dim(value, index, dim, keepdims=False).astype(F32)
    for s in range(1, size):
        leaving = lax.dynamic_index_in_dim(value, (index - s) % size, dim, keepdims=False)
        total = total + shift_by(leaving.astype(BF16), axis, -s).astype(F32)
    return total


def rows_gathered(block):
    value = in_order(pieces_of(block, "a"), "a", 0)
    value = in_order(pieces_of(value, "b"), "b", 1)
    value = in_order(pieces_of(value, "c"), "c", 2)
    return value.reshape(-1, block.shape[-1])


def rows_scattered(partial):
    sizes = tuple(lax.axis_size(n) for n in ("a", "b", "c"))
    width = partial.shape[1]
    value = partial.reshape(*sizes, -1, width)
    value = scatter_sum(value, "c", 2)
    value = scatter_sum(value, "b", 1)
    value = scatter_sum(value, "a", 0)
    count = lax.axis_size("z")
    local = width // count
    total = value[:, :local]
    for s in range(1, count):
        total = total + shift_by(value[:, s * local : (s + 1) * local].astype(BF16), "z", -s).astype(F32)
    return total


def swapped(block):
    count = lax.axis_size("z")
    return lax.ppermute(
        block,
        ("b", "c", "z"),
        [(t * count + z, z * count + t) for t in range(count) for z in range(count)],
    )


def team_gathered(value):
    near = pieces_of(value, "b")
    far = shift_by(jnp.concatenate(near, axis=0), "c", 1)
    return jnp.concatenate([*near, far], axis=0)


def team_scattered(partial):
    half = partial.shape[0] // 2
    value = partial[:half] + shift_by(partial[half:].astype(BF16), "c", 1).astype(F32)
    count = lax.axis_size("b")
    size = half // count
    total = value[:size]
    for s in range(1, count):
        total = total + shift_by(value[s * size : (s + 1) * size].astype(BF16), "b", -s).astype(F32)
    return total


def per_device(
    tokens,
    lengths,
    permutation,
    cotangent,
    norm1_gain,
    mixer_in,
    mixer_gate,
    conv_kernel,
    mixer_out,
    norm2_gain,
    ffn_gate,
    ffn_up,
    ffn_down,
):
    micro, length, width = tokens.shape
    count_b, count_z = lax.axis_size("b"), lax.axis_size("z")
    ia, ib, ic, iz = (lax.axis_index(n) for n in EVERY)
    place = ((ia * count_b + ib) * 2 + ic) * count_z + iz
    per_block = BLOCK // length
    blocks = permutation.shape[1]
    local = conv_kernel.shape[1]
    rows = micro * length

    ffn_g, ffn_u, ffn_d = (
        lax.all_gather(swapped(w), ("a", "z"), axis=0, tiled=True) for w in (ffn_gate, ffn_up, ffn_down)
    )
    both = jnp.concatenate(
        [*pieces_of(mixer_in, "z"), *pieces_of(mixer_gate, "z")], axis=1
    )
    both = rows_gathered(both)
    w_out = rows_gathered(jnp.concatenate(pieces_of(mixer_out, "z"), axis=1))
    kernel = jnp.concatenate(pieces_of(conv_kernel, "z"), axis=1)
    cot_team = team_gathered(cotangent.reshape(rows, width))

    dealt = lax.dynamic_slice_in_dim(permutation, place // per_block, 1, axis=1)[:, 0]
    own = dealt * per_block + place % per_block
    spots = jnp.arange(blocks, dtype=jnp.int32)

    def holder(piece):
        at = jnp.sum(jnp.where(permutation == (piece // per_block)[:, None], spots[None, :], 0), axis=1)
        return at * per_block + piece % per_block

    before = holder(jnp.maximum(own - 1, 0))
    last = blocks * per_block - 1
    after = holder(jnp.minimum(own + 1, last))
    order = jnp.arange(lengths.shape[1], dtype=jnp.int32)
    offsets = jnp.sum(jnp.where(order[None, None, :] < order[None, :, None], lengths[:, None, :], 0), axis=2)
    position = own[:, None] * length + jnp.arange(length, dtype=jnp.int32)[None, :]
    is_start = jnp.any(position[:, :, None] == offsets[:, None, :], axis=2)
    was_start = jnp.any(position[:, :, None] - 1 == offsets[:, None, :], axis=2)
    keep_one = jnp.where(is_start, 0.0, 1.0).astype(F32)[:, :, None]
    keep_two = jnp.where(is_start | was_start, 0.0, 1.0).astype(F32)[:, :, None]

    def pick(everyone, source):
        return jnp.stack(
            [
                lax.dynamic_slice(everyone, (source[m], m, 0, 0), (1, 1, 2, everyone.shape[3]))[0, 0]
                for m in range(micro)
            ]
        )

    tails = pick(lax.all_gather(tokens[:, length - 2 :, :], EVERY, axis=0), before)
    local_in = tokens.reshape(rows, width).astype(F32)
    local_cot = cotangent.reshape(rows, width).astype(F32)
    scale_one = lax.rsqrt(jnp.mean(local_in * local_in, axis=1, keepdims=True) + EPSILON)
    normed_one = local_in * scale_one
    hidden_one = (normed_one * norm1_gain).astype(BF16)
    tail_in = tails.reshape(micro * 2, width).astype(F32)
    tail_scale = lax.rsqrt(jnp.mean(tail_in * tail_in, axis=1, keepdims=True) + EPSILON)
    tail_hidden = (tail_in * tail_scale * norm1_gain).astype(BF16)
    channels = kernel.shape[1]
    signal_gating = dot_nn(hidden_one, both)
    signal = signal_gating[:, :channels].reshape(micro, length, channels)
    gating = signal_gating[:, channels:].reshape(micro, length, channels)
    tail_signal = dot_nn(tail_hidden, both[:, :channels]).reshape(micro, 2, channels)
    extended = jnp.concatenate([tail_signal, signal], axis=1)
    shift_one = keep_one * extended[:, 1 : length + 1, :]
    shift_two = keep_two * extended[:, 0:length, :]
    mixed = kernel[0] * signal + kernel[1] * shift_one + kernel[2] * shift_two
    product = (mixed * gating).astype(BF16).reshape(rows, channels)
    residual = local_in + dot_nt(product, w_out)

    scale_two = lax.rsqrt(jnp.mean(residual * residual, axis=1, keepdims=True) + EPSILON)
    normed_two = residual * scale_two
    hidden_two = team_gathered((normed_two * norm2_gain).astype(BF16))
    gate_val = dot_nn(hidden_two, ffn_g)
    up_val = dot_nn(hidden_two, ffn_u)
    sigmoid_gate = jax.nn.sigmoid(gate_val)
    activated = (gate_val * sigmoid_gate * up_val).astype(BF16)
    output = (residual + team_scattered(dot_nt(activated, ffn_d))).astype(BF16)

    def ffn_scattered(partial):
        value = partial.reshape(2, count_z, -1, partial.shape[1])
        value = scatter_sum(value, "a", 0)
        value = scatter_sum(value, "z", 0)
        return swapped(value.astype(BF16)).astype(F32)

    grad_down = ffn_scattered(dot_tn(cot_team, activated).astype(BF16))
    grad_act = dot_nn(cot_team, ffn_d)
    slope = sigmoid_gate * (1.0 + gate_val * (1.0 - sigmoid_gate))
    grad_gate = (grad_act * up_val * slope).astype(BF16)
    grad_up = (grad_act * gate_val * sigmoid_gate).astype(BF16)
    grad_hidden_two = team_scattered(dot_nt(grad_gate, ffn_g) + dot_nt(grad_up, ffn_u))
    grad_ffg = ffn_scattered(dot_tn(hidden_two, grad_gate).astype(BF16))
    grad_ffu = ffn_scattered(dot_tn(hidden_two, grad_up).astype(BF16))

    grad_gain_two = jnp.sum(grad_hidden_two * normed_two, axis=0)
    grad_norm_two = grad_hidden_two * norm2_gain
    inner_two = jnp.mean(grad_norm_two * normed_two, axis=1, keepdims=True)
    grad_residual = local_cot + scale_two * (grad_norm_two - normed_two * inner_two)
    grad_branch = grad_residual.astype(BF16)
    grad_product = dot_nn(grad_branch, w_out).reshape(micro, length, channels)
    grad_out = rows_scattered(dot_tn(grad_branch, product).astype(BF16))
    grad_mixed = grad_product * gating
    grad_gating = (grad_product * mixed).astype(BF16).reshape(rows, channels)
    grad_kernel = jnp.stack(
        [
            jnp.sum(grad_mixed * signal, axis=(0, 1)),
            jnp.sum(grad_mixed * shift_one, axis=(0, 1)),
            jnp.sum(grad_mixed * shift_two, axis=(0, 1)),
        ]
    )
    into_one = kernel[1] * (keep_one * grad_mixed)
    into_two = kernel[2] * (keep_two * grad_mixed)
    leaving = jnp.stack([into_two[:, 0], into_one[:, 0] + into_two[:, 1]], axis=1)
    blocked = leaving.reshape(micro, 2, count_z, local)

    def turned(value, dim):
        picks = [
            lax.dynamic_index_in_dim(value, (iz - j) % count_z, dim, keepdims=False) for j in range(count_z)
        ]
        return jnp.concatenate(picks, axis=-1)

    everyone = lax.all_gather(turned(blocked, 2).astype(BF16), EVERY, axis=0)
    arrived = turned(pick(everyone, after).reshape(micro, 2, count_z, local), 2).astype(F32)
    arrived = jnp.where((own == last)[:, None, None], 0.0, arrived)
    from_one = jnp.concatenate([into_one[:, 1:], arrived[:, 1:]], axis=1)
    from_two = jnp.concatenate([into_two[:, 2:], arrived[:, :1], jnp.zeros_like(arrived[:, :1])], axis=1)
    grad_signal = (kernel[0] * grad_mixed + from_one + from_two).astype(BF16).reshape(rows, channels)
    grad_gate_w = rows_scattered(dot_tn(hidden_one, grad_gating).astype(BF16))
    grad_in_w = rows_scattered(dot_tn(hidden_one, grad_signal).astype(BF16))
    grad_hidden_one = dot_nt(jnp.concatenate([grad_signal, grad_gating], axis=1), both)
    grad_gain_one = jnp.sum(grad_hidden_one * normed_one, axis=0)
    grad_norm_one = grad_hidden_one * norm1_gain
    inner_one = jnp.mean(grad_norm_one * normed_one, axis=1, keepdims=True)
    input_grad = grad_residual + scale_one * (grad_norm_one - normed_one * inner_one)

    row_count = 4 * count_b
    kernel_parts = turned(grad_kernel.reshape(3, count_z, local), 1).reshape(3, count_z, row_count, -1)
    small = jnp.concatenate(
        [
            grad_gain_one.reshape(row_count, count_z, 1, -1),
            grad_gain_two.reshape(row_count, count_z, 1, -1),
            kernel_parts.transpose(2, 1, 0, 3),
        ],
        axis=2,
    ).reshape(row_count * count_z, 5, -1)
    small = lax.psum_scatter(small, EVERY, scatter_dimension=0, tiled=True)[0]
    return (
        output.reshape(micro, length, width),
        input_grad.reshape(micro, length, width),
        small[0],
        grad_in_w,
        grad_gate_w,
        small[2:5],
        grad_out,
        small[1],
        grad_ffg,
        grad_ffu,
        grad_down,
    )


def solution(mesh):
    row, col = mesh.shape["row"], mesh.shape["col"]
    fine = Mesh(mesh.devices.reshape(2, row // 4, 2, col), EVERY)
    by_rows = ("a", "b", "c")
    matrix = P(by_rows, "z")
    token = P(None, EVERY, None)
    return jax.shard_map(
        per_device,
        mesh=fine,
        in_specs=(
            token,
            P(),
            P(),
            token,
            P(),
            matrix,
            matrix,
            P(None, "z"),
            matrix,
            P(),
            matrix,
            matrix,
            matrix,
        ),
        out_specs=(
            token,
            token,
            P(EVERY),
            matrix,
            matrix,
            P(None, ("z", *by_rows)),
            matrix,
            P(EVERY),
            matrix,
            matrix,
            matrix,
        ),
        check_vma=False,
    )
```

```python
import functools

import jax
import jax.numpy as jnp
from jax import lax
from jax.experimental import pallas as pl
from jax.experimental.pallas import tpu as pltpu
from jax.sharding import Mesh
from jax.sharding import PartitionSpec as P

BLOCK = 128
EPSILON = 1e-05
F32 = jnp.float32
BF16 = jnp.bfloat16
EVERY = ("a", "b", "c", "z")


def dot_nn(left, right):
    return lax.dot_general(left, right, (((1,), (0,)), ((), ())), preferred_element_type=F32)


def dot_nt(left, right):
    return lax.dot_general(left, right, (((1,), (1,)), ((), ())), preferred_element_type=F32)


def dot_tn(left, right):
    return lax.dot_general(left, right, (((0,), (0,)), ((), ())), preferred_element_type=F32)


def shift_by(value, axis, amount):
    size = lax.axis_size(axis)
    return lax.ppermute(value, axis, [(i, (i + amount) % size) for i in range(size)])


def pieces_of(value, axis):
    return [value] + [shift_by(value, axis, s) for s in range(1, lax.axis_size(axis))]


def near_pieces(value, axis):
    return shift_by(value, axis, 1), shift_by(value, axis, -1)


def far_pieces(value, near, axis):
    size = lax.axis_size(axis)
    pieces = [value] + [None] * (size - 1)
    pieces[1], pieces[size - 1] = near
    for s in range(2, size // 2 + 1):
        pieces[s] = shift_by(pieces[s - 1], axis, 1)
    for s in range(2, (size - 1) // 2 + 1):
        pieces[size - s] = shift_by(pieces[size - s + 1], axis, -1)
    return pieces


def phase(*values):
    return lax.optimization_barrier(values)


def after(value, *earlier):
    return lax.optimization_barrier((value, earlier))[0]


def in_order(pieces, axis, dim):
    size, index = len(pieces), lax.axis_index(axis)
    if size == 2:
        first = index == 0
        return jnp.stack(
            [jnp.where(first, pieces[0], pieces[1]), jnp.where(first, pieces[1], pieces[0])], axis=dim
        )
    return jnp.stack(
        [lax.select_n((index - j) % size, *pieces) for j in range(size)], axis=dim
    )


def parted(terms, axis, dim):
    size, index = lax.axis_size(axis), lax.axis_index(axis)

    def slices(i):
        return [lax.dynamic_index_in_dim(t, i, dim, keepdims=False) for t in terms]

    return slices(index) + [
        shift_by(joined(slices((index - s) % size)).astype(BF16), axis, -s) for s in range(1, size)
    ]


def joined(terms):
    total = terms[0].astype(F32)
    for value in terms[1:]:
        total = total + value.astype(F32)
    return total


def columns_home(terms):
    count = lax.axis_size("z")
    local = terms[0].shape[1] // count

    def columns(s):
        return joined([t[:, s * local : (s + 1) * local] for t in terms])

    return [columns(0)] + [shift_by(columns(s).astype(BF16), "z", -s) for s in range(1, count)]


def swapped(block, back=False):
    count, size = lax.axis_size("z"), lax.axis_size("b")
    moves = []
    for t in range(count):
        for z in range(count):
            team = (z % size) * 2 + z // size
            moves.append((t * count + z, team * count + t))
    return lax.ppermute(block, ("b", "c", "z"), [(j, i) if back else (i, j) for i, j in moves])


def partner(value, bit):
    count = lax.axis_size(EVERY)
    return lax.ppermute(value, EVERY, [(i, i ^ bit) for i in range(count)])


def exchange_order():
    bits = [1 << i for i in range(lax.axis_size(EVERY).bit_length() - 1)]
    core = lax.axis_size("z")
    return [b for b in bits[::-1] if b > core] + [b for b in bits if b < core] + [core]


def entry_of(difference):
    return sum(((difference & bit) // bit) << i for i, bit in enumerate(exchange_order()))


def told(value, bits):
    for bit in bits:
        value = jnp.concatenate([value, partner(value, bit)], axis=0)
    return value


def middle_kernel(steps, *refs):
    near_hidden, far_hidden, near_cot, far_cot, w_gate, w_up, w_down = refs[:7]
    activated, grads, near_back, far_back, near_out, far_out = refs[-6:]
    units = w_down.shape[1]
    near = pl.program_id(0) < steps
    hidden = jnp.where(near, near_hidden[...], far_hidden[...])
    cot = jnp.where(near, near_cot[...], far_cot[...])
    gate = dot_nn(hidden, w_gate[...])
    up = dot_nn(hidden, w_up[...])
    grad = dot_nn(cot, w_down[...])
    sigmoid = 1.0 / (1.0 + jnp.exp(-gate))
    silu = gate * sigmoid
    active = (silu * up).astype(BF16)
    to_gate = (grad * up * (sigmoid * (1.0 + gate * (1.0 - sigmoid)))).astype(BF16)
    to_up = (grad * silu).astype(BF16)
    activated[...] = active
    grads[:, :units] = to_gate
    grads[:, units:] = to_up
    back = (dot_nt(to_gate, w_gate[...]) + dot_nt(to_up, w_up[...])).astype(BF16)
    out = dot_nt(active, w_down[...]).astype(BF16)

    @pl.when(near)
    def _():
        near_back[...] = back
        near_out[...] = out

    @pl.when(jnp.logical_not(near))
    def _():
        far_back[...] = back
        far_out[...] = out


def middle(part, parts, hidden, cot, w_gate, w_up, w_down, held):
    rows, width = hidden[0].shape
    units = w_down.shape[1]
    tile = min(rows, 256)
    steps = rows // tile
    near = pl.BlockSpec((tile, width), lambda i: (jnp.minimum(i, steps - 1), 0))
    far = pl.BlockSpec((tile, width), lambda i: (jnp.maximum(i - steps, 0), 0))
    weight = pl.BlockSpec((width, units), lambda i: (0, 0), pipeline_mode=pl.Buffered(1))
    results = [pl.BlockSpec((tile, n * units), lambda i: (part * 2 * steps + i, 0)) for n in (1, 2)]
    return pl.pallas_call(
        functools.partial(middle_kernel, steps),
        grid=(2 * steps,),
        in_specs=[near, far, near, far, weight, weight, weight]
        + [pl.BlockSpec(memory_space=pl.ANY)] * len(held),
        out_specs=results + [near, far] * 2,
        out_shape=[jax.ShapeDtypeStruct((parts * 2 * rows, n * units), BF16) for n in (1, 2)]
        + [jax.ShapeDtypeStruct((rows, width), BF16)] * 4,
        input_output_aliases={7 + i: i for i in range(len(held))},
        compiler_params=pltpu.CompilerParams(vmem_limit_bytes=58 * 2**20),
        cost_estimate=pl.CostEstimate(
            flops=24 * rows * width * units,
            bytes_accessed=2 * (8 * rows * width + 3 * width * units + 6 * rows * units),
            transcendentals=2 * rows * units,
        ),
        name="middle",
    )(*hidden, *cot, w_gate, w_up, w_down, *held)


def gradient_kernel(*refs, count, extra):
    side, tokens, right, result = refs[0], refs[1 : 1 + count], refs[1 + count], refs[-1]
    del side
    rows = tokens[0].shape[0]
    total = refs[2 + count][...].astype(F32) if extra else None
    for i in range(count):
        term = lax.dot_general(
            tokens[i][...], right[i * rows : (i + 1) * rows, :], (((0,), (0,)), ((), ())), preferred_element_type=F32
        )
        total = term if total is None else total + term
    result[...] = total.astype(BF16)


def gradient_half(side, tokens, right, units, column=0, extra=()):
    rows, width = tokens[0].shape
    count, half = len(tokens), width // 2
    tile = 256 if units % 256 == 0 else 128
    steps = units // tile
    out = pl.BlockSpec((half, tile), lambda j, side: (0, j))
    return pl.pallas_call(
        functools.partial(gradient_kernel, count=count, extra=len(extra)),
        grid_spec=pltpu.PrefetchScalarGridSpec(
            num_scalar_prefetch=1,
            grid=(steps,),
            in_specs=[
                pl.BlockSpec((rows, half), lambda j, side: (0, side[0]), pipeline_mode=pl.Buffered(1))
            ]
            * count
            + [pl.BlockSpec((count * rows, tile), lambda j, side: (0, column * steps + j))]
            + [out] * len(extra),
            out_specs=out,
        ),
        out_shape=jax.ShapeDtypeStruct((half, units), BF16),
        compiler_params=pltpu.CompilerParams(vmem_limit_bytes=40 * 2**20),
        cost_estimate=pl.CostEstimate(
            flops=2 * count * rows * half * units,
            bytes_accessed=2 * (count * rows * (half + units) + half * units),
            transcendentals=0,
        ),
        name="gradient_half",
    )(side.reshape(1).astype(jnp.int32), *tokens, right, *extra)


def split_kernel(core, left, right, kept, leaving):
    total = lax.dot_general(left[...], right[...], (((0,), (0,)), ((), ())), preferred_element_type=F32)
    groups, _, rows, _ = (kept.shape[0], 2, *kept.shape[1:])
    total = total.astype(BF16).reshape(groups, 2, rows, -1)
    first = core[0] == 0
    kept[...] = jnp.where(first, total[:, 0], total[:, 1])
    leaving[...] = jnp.where(first, total[:, 1], total[:, 0])


def split_gradient(core, left, right, groups):
    count, width = left.shape
    columns = right.shape[1]
    tile = 256
    rows = width // (2 * groups)
    out = pl.BlockSpec((groups, rows, tile), lambda j, core: (0, 0, j))
    return pl.pallas_call(
        split_kernel,
        grid_spec=pltpu.PrefetchScalarGridSpec(
            num_scalar_prefetch=1,
            grid=(columns // tile,),
            in_specs=[
                pl.BlockSpec((count, width), lambda j, core: (0, 0), pipeline_mode=pl.Buffered(1)),
                pl.BlockSpec((count, tile), lambda j, core: (0, j)),
            ],
            out_specs=[out, out],
        ),
        out_shape=[jax.ShapeDtypeStruct((groups, rows, columns), BF16)] * 2,
        compiler_params=pltpu.CompilerParams(vmem_limit_bytes=40 * 2**20),
        cost_estimate=pl.CostEstimate(
            flops=2 * count * width * columns,
            bytes_accessed=2 * (count * (width + columns) + width * columns),
            transcendentals=0,
        ),
        name="split_gradient",
    )(core.reshape(1).astype(jnp.int32), left, right)


def per_device(
    tokens,
    lengths,
    permutation,
    cotangent,
    norm1_gain,
    mixer_in,
    mixer_gate,
    conv_kernel,
    mixer_out,
    norm2_gain,
    ffn_gate,
    ffn_up,
    ffn_down,
):
    micro, length, width = tokens.shape
    count_b, count_z = lax.axis_size("b"), lax.axis_size("z")
    ia, ib, ic, iz = (lax.axis_index(n) for n in EVERY)
    place = ((ia * count_b + ib) * 2 + ic) * count_z + iz
    per_block = BLOCK // length
    blocks = permutation.shape[1]
    local = conv_kernel.shape[1]
    rows = micro * length

    dealt = lax.dynamic_slice_in_dim(permutation, place // per_block, 1, axis=1)[:, 0]
    own = dealt * per_block + place % per_block
    spots = jnp.arange(blocks, dtype=jnp.int32)

    def holder(piece):
        at = jnp.sum(jnp.where(permutation == (piece // per_block)[:, None], spots[None, :], 0), axis=1)
        return at * per_block + piece % per_block

    before = holder(jnp.maximum(own - 1, 0))
    last = blocks * per_block - 1
    behind = holder(jnp.minimum(own + 1, last))
    order = jnp.arange(lengths.shape[1], dtype=jnp.int32)
    offsets = jnp.sum(jnp.where(order[None, None, :] < order[None, :, None], lengths[:, None, :], 0), axis=2)
    position = own[:, None] * length + jnp.arange(length, dtype=jnp.int32)[None, :]
    is_start = jnp.any(position[:, :, None] == offsets[:, None, :], axis=2)
    was_start = jnp.any(position[:, :, None] - 1 == offsets[:, None, :], axis=2)
    keep_one = jnp.where(is_start, 0.0, 1.0).astype(F32)[:, :, None]
    keep_two = jnp.where(is_start | was_start, 0.0, 1.0).astype(F32)[:, :, None]

    units = -(-ffn_gate.shape[1] // 128) * 128
    spare = ((0, 0), (0, units - ffn_gate.shape[1]))

    def rows_of(pieces):
        return lax.all_gather(jnp.concatenate(pieces, axis=1), ("a", "b", "c"), axis=0, tiled=True)

    def told_at_once(value):
        return lax.all_gather(lax.all_gather(value, "z", axis=0), ("a", "b", "c"), axis=0)

    bits = exchange_order()
    hops = [tuple(bits[:-3]), *((b,) for b in bits[-3:])]
    tails = told(tokens[:, length - 2 :, :].reshape(1, micro * 2, width), hops[0])
    z_in = pieces_of(mixer_in, "z")
    taps = pieces_of(conv_kernel, "z")
    z_in, tails, taps, mixer_gate, ffn_gate_later, mixer_out = phase(
        z_in, tails, taps, mixer_gate, ffn_gate, mixer_out
    )
    w_in = rows_of(z_in)
    z_gate = pieces_of(mixer_gate, "z")
    swap_g = swapped(jnp.pad(ffn_gate_later, spare))
    tails = told(tails, hops[1])
    z_gate, swap_g, tails, mixer_out, ffn_up_later, ffn_down, cotangent_later = phase(
        z_gate, swap_g, tails, mixer_out, ffn_up, ffn_down, cotangent
    )
    w_gate = rows_of(z_gate)
    z_out = pieces_of(mixer_out, "z")
    near_g = near_pieces(swap_g, "z")
    tails = told(tails, hops[2])
    z_out, near_g, tails, cotangent_later, ffn_up_later, ffn_down, w_in = phase(
        z_out, near_g, tails, cotangent_later, ffn_up_later, ffn_down, w_in
    )
    w_out = rows_of(z_out)
    z_g = far_pieces(swap_g, near_g, "z")
    swap_u, swap_d = swapped(jnp.pad(ffn_up_later, spare)), swapped(jnp.pad(ffn_down, spare))
    tails = told(tails, hops[3])
    z_g, swap_u, swap_d, cotangent_later, tails, w_gate = phase(z_g, swap_u, swap_d, cotangent_later, tails, w_gate)
    y_g = pieces_of(in_order(z_g, "z", 0), "a")
    z_u = pieces_of(swap_u, "z")
    y_d = pieces_of(swap_d, "a")
    far_cotangent = pieces_of(cotangent_later.reshape(rows, width), "b")
    kernel = jnp.concatenate(taps, axis=1)

    tail_in = jnp.concatenate(
        [
            lax.dynamic_slice(tails, (entry_of(before[m] ^ place), 2 * m, 0), (1, 2, width))[0]
            for m in range(micro)
        ]
    ).astype(F32)
    local_in = tokens.reshape(rows, width).astype(F32)
    local_cot = cotangent.reshape(rows, width).astype(F32)
    scale_one = lax.rsqrt(jnp.mean(local_in * local_in, axis=1, keepdims=True) + EPSILON)
    normed_one = local_in * scale_one
    hidden_one = (normed_one * norm1_gain).astype(BF16)
    tail_scale = lax.rsqrt(jnp.mean(tail_in * tail_in, axis=1, keepdims=True) + EPSILON)
    tail_hidden = (tail_in * tail_scale * norm1_gain).astype(BF16)
    channels = kernel.shape[1]
    signal = dot_nn(hidden_one, w_in).reshape(micro, length, channels)
    tail_signal = dot_nn(tail_hidden, w_in).reshape(micro, 2, channels)
    gating = dot_nn(hidden_one, w_gate).reshape(micro, length, channels)
    extended = jnp.concatenate([tail_signal, signal], axis=1)
    shift_one = keep_one * extended[:, 1 : length + 1, :]
    shift_two = keep_two * extended[:, 0:length, :]
    mixed = kernel[0] * signal + kernel[1] * shift_one + kernel[2] * shift_two
    product = (mixed * gating).astype(BF16).reshape(rows, channels)
    residual = local_in + dot_nt(product, w_out)

    scale_two = lax.rsqrt(jnp.mean(residual * residual, axis=1, keepdims=True) + EPSILON)
    normed_two = residual * scale_two
    hidden_own = (normed_two * norm2_gain).astype(BF16)

    y_g, z_u, y_d, far_cotangent, hidden_own = phase(y_g, z_u, y_d, far_cotangent, hidden_own)
    half_d = in_order(y_d, "a", 0)
    near_d = near_pieces(half_d, "z")
    y_u = pieces_of(in_order(z_u, "z", 0), "a")
    ffn_g = in_order(y_g, "a", 0).reshape(-1, units)

    def with_core(pieces):
        return [v for piece in pieces for v in (piece, shift_by(piece, "c", 1))]

    cot_parts = with_core(far_cotangent)
    hidden_parts = with_core([hidden_own])
    far_hidden = pieces_of(hidden_own, "b")[1:]
    near_d, y_u, half_d, ffn_g, cot_parts, hidden_parts, far_hidden = phase(
        near_d, y_u, half_d, ffn_g, cot_parts, hidden_parts, far_hidden
    )
    ffn_d = in_order(far_pieces(half_d, near_d, "z"), "z", 1).reshape(-1, units)
    ffn_u = in_order(y_u, "a", 0).reshape(-1, units)
    hidden_parts = hidden_parts + with_core(far_hidden)
    held, backs, outs = (), [], []
    for s in range(count_b):
        pair = slice(2 * s, 2 * s + 2)
        *held, near_back, far_back, near_out, far_out = middle(
            s, count_b, hidden_parts[pair], cot_parts[pair], ffn_g, ffn_u, ffn_d, held
        )
        backs.append((near_back, shift_by(far_back, "c", 1)))
        outs.append((near_out, shift_by(far_out, "c", 1)))
    activated, grads = held

    other = 1 - ia

    def to_owners(sums):
        return [(near.astype(F32) + far.astype(F32)).astype(BF16) for near, far in sums[1:]]

    def passed(values):
        return [shift_by(v, "b", -1 - i) for i, v in enumerate(values)]

    leaving_gate = gradient_half(other, hidden_parts, grads, units)
    leaving_gate, backs, outs, hidden_parts, cot_parts = phase(leaving_gate, backs, outs, hidden_parts, cot_parts)
    come_gate, came_back = shift_by(leaving_gate, "a", 1), passed(to_owners(backs))
    leaving_up = gradient_half(other, hidden_parts, grads, units, 1)
    leaving_down = gradient_half(other, cot_parts, activated, units)
    stay_gate = gradient_half(ia, hidden_parts, grads, units)
    stay_up = gradient_half(ia, hidden_parts, grads, units, 1)
    stay_down = gradient_half(ia, cot_parts, activated, units)
    leaving_out = to_owners(outs)
    come_gate, came_back, leaving_up, leaving_down, stay_gate, stay_up, stay_down, outs, leaving_out = phase(
        come_gate, came_back, leaving_up, leaving_down, stay_gate, stay_up, stay_down, outs, leaving_out
    )
    come_up, came_out = shift_by(leaving_up, "a", 1), passed(leaving_out)

    def over_z(stay, come):
        return lax.psum_scatter(joined([stay, come]).astype(BF16), "z", scatter_dimension=0, tiled=True)

    grad_hidden_two = joined([*backs[0], *came_back])

    grad_gain_two = jnp.sum(grad_hidden_two * normed_two, axis=0)
    grad_norm_two = grad_hidden_two * norm2_gain
    inner_two = jnp.mean(grad_norm_two * normed_two, axis=1, keepdims=True)
    grad_residual = local_cot + scale_two * (grad_norm_two - normed_two * inner_two)
    grad_branch = grad_residual.astype(BF16)
    grad_product = dot_nn(grad_branch, w_out).reshape(micro, length, channels)
    def over_c(split):
        kept, leaving = split
        shape = (2, count_b, *kept.shape[1:])
        return [kept.reshape(shape), shift_by(leaving, "c", 1).reshape(shape)]

    def split(left, right):
        return split_gradient(ic, left, right, 2 * count_b)

    out_split = split(grad_branch, product)
    grad_mixed = grad_product * gating
    grad_gating = (grad_product * mixed).astype(BF16).reshape(rows, channels)
    grad_kernel = jnp.stack(
        [
            jnp.sum(grad_mixed * signal, axis=(0, 1)),
            jnp.sum(grad_mixed * shift_one, axis=(0, 1)),
            jnp.sum(grad_mixed * shift_two, axis=(0, 1)),
        ]
    )
    into_one = kernel[1] * (keep_one * grad_mixed)
    into_two = kernel[2] * (keep_two * grad_mixed)
    leaving = jnp.stack([into_two[:, 0], into_one[:, 0] + into_two[:, 1]], axis=1)
    blocked = leaving.reshape(micro, 2, count_z, local)

    def turned(value, dim):
        picks = [
            lax.dynamic_index_in_dim(value, (iz - j) % count_z, dim, keepdims=False) for j in range(count_z)
        ]
        return jnp.concatenate(picks, axis=-1)

    blocked = turned(blocked, 2).reshape(micro * 2, channels).astype(BF16)
    gate_split = split(hidden_one, grad_gating)
    blocked, come_up, came_out, out_split, gate_split, grad_mixed, leaving_down = phase(
        blocked, come_up, came_out, out_split, gate_split, grad_mixed, leaving_down
    )
    everyone = told_at_once(blocked)
    out_c, gate_c = over_c(out_split), over_c(gate_split)
    everyone, out_c, gate_c, grad_mixed, leaving_down, come_gate, come_up = phase(
        everyone, out_c, gate_c, grad_mixed, leaving_down, come_gate, come_up
    )

    def over_z(stay, come):
        return lax.psum_scatter(joined([stay, come]).astype(BF16), "z", scatter_dimension=0, tiled=True)

    come_down = shift_by(leaving_down, "a", 1)
    out_b = parted(out_c, "b", 1)
    scattered_gate, scattered_up = over_z(stay_gate, come_gate), over_z(stay_up, come_up)
    into_one = kernel[1] * (keep_one * grad_mixed)
    into_two = kernel[2] * (keep_two * grad_mixed)
    arrived = jnp.stack(
        [
            lax.dynamic_slice(
                everyone, (behind[m] // count_z, behind[m] % count_z, 2 * m, 0), (1, 1, 2, channels)
            )[0, 0]
            for m in range(micro)
        ]
    )
    arrived = turned(arrived.reshape(micro, 2, count_z, local), 2).astype(F32)
    arrived = jnp.where((own == last)[:, None, None], 0.0, arrived)
    from_one = jnp.concatenate([into_one[:, 1:], arrived[:, 1:]], axis=1)
    from_two = jnp.concatenate([into_two[:, 2:], arrived[:, :1], jnp.zeros_like(arrived[:, :1])], axis=1)
    grad_signal = (kernel[0] * grad_mixed + from_one + from_two).astype(BF16).reshape(rows, channels)
    in_split = split(hidden_one, grad_signal)
    grad_hidden_one = dot_nt(grad_signal, w_in) + dot_nt(grad_gating, w_gate)
    grad_gain_one = jnp.sum(grad_hidden_one * normed_one, axis=0)
    grad_norm_one = grad_hidden_one * norm1_gain
    inner_one = jnp.mean(grad_norm_one * normed_one, axis=1, keepdims=True)
    input_grad = grad_residual + scale_one * (grad_norm_one - normed_one * inner_one)
    come_down, out_b, in_split, gate_c, input_grad, scattered_gate, grad_gain_one, outs = phase(
        come_down, out_b, in_split, gate_c, input_grad, scattered_gate, grad_gain_one, outs
    )
    in_c = over_c(in_split)
    gate_b = parted(gate_c, "b", 1)
    out_a = parted(out_b, "a", 0)
    gate_home = swapped(scattered_gate, True)
    scattered_down = over_z(stay_down, come_down)
    output = (joined([*outs[0], *came_out]) + residual).astype(BF16)
    in_c, gate_b, out_a, gate_home, scattered_up, output = phase(
        in_c, gate_b, out_a, gate_home, scattered_up, output
    )
    in_b = parted(in_c, "b", 1)
    gate_a = parted(gate_b, "a", 0)
    out_z = columns_home(out_a)
    up_home = swapped(scattered_up, True)
    in_b, gate_a, out_z, up_home, scattered_down = phase(in_b, gate_a, out_z, up_home, scattered_down)
    in_a = parted(in_b, "a", 0)
    gate_z = columns_home(gate_a)
    down_home = swapped(scattered_down, True)
    small = jnp.concatenate(
        [grad_gain_one[None], grad_gain_two[None], turned(grad_kernel.reshape(3, count_z, local), 1)]
    )
    small = lax.all_gather(after(small, scattered_down), EVERY, axis=0)
    in_a, gate_z, down_home = phase(in_a, gate_z, down_home)
    in_z = columns_home(in_a)
    share = width // (4 * count_b * count_z)
    gains = lax.dynamic_slice_in_dim(small[:, :2], place * share, share, axis=2)
    tap_grads = lax.dynamic_slice_in_dim(
        small[:, 2:], (iz * 4 * count_b + place // count_z) * share, share, axis=2
    )
    gains, tap_grads = jnp.sum(gains, axis=0), jnp.sum(tap_grads, axis=0)
    grad_out, grad_gate_w, grad_in_w = (joined(t) for t in (out_z, gate_z, in_z))
    hidden_units = ffn_gate.shape[1]
    grad_ffg, grad_ffu, grad_down = (g[:, :hidden_units].astype(F32) for g in (gate_home, up_home, down_home))

    return (
        output.reshape(micro, length, width),
        input_grad.reshape(micro, length, width),
        gains[0],
        grad_in_w,
        grad_gate_w,
        tap_grads,
        grad_out,
        gains[1],
        grad_ffg,
        grad_ffu,
        grad_down,
    )


def solution(mesh):
    row, col = mesh.shape["row"], mesh.shape["col"]
    fine = Mesh(mesh.devices.reshape(2, row // 4, 2, col), EVERY)
    by_rows = ("a", "b", "c")
    matrix = P(by_rows, "z")
    token = P(None, EVERY, None)
    return jax.shard_map(
        per_device,
        mesh=fine,
        in_specs=(
            token,
            P(),
            P(),
            token,
            P(),
            matrix,
            matrix,
            P(None, "z"),
            matrix,
            P(),
            matrix,
            matrix,
            matrix,
        ),
        out_specs=(
            token,
            token,
            P(EVERY),
            matrix,
            matrix,
            P(None, ("z", *by_rows)),
            matrix,
            P(EVERY),
            matrix,
            matrix,
            matrix,
        ),
        check_vma=False,
    )
```

```python
import functools

import jax
import jax.numpy as jnp
from jax import lax
from jax.experimental import pallas as pl
from jax.experimental.pallas import tpu as pltpu
from jax.sharding import Mesh
from jax.sharding import PartitionSpec as P

BLOCK = 128
EPSILON = 1e-05
F32 = jnp.float32
BF16 = jnp.bfloat16
EVERY = ("a", "b", "c", "z")


def dot_nn(left, right):
    return lax.dot_general(left, right, (((1,), (0,)), ((), ())), preferred_element_type=F32)


def dot_nt(left, right):
    return lax.dot_general(left, right, (((1,), (1,)), ((), ())), preferred_element_type=F32)


def dot_tn(left, right):
    return lax.dot_general(left, right, (((0,), (0,)), ((), ())), preferred_element_type=F32)


def shift_by(value, axis, amount):
    size = lax.axis_size(axis)
    return lax.ppermute(value, axis, [(i, (i + amount) % size) for i in range(size)])


def pieces_of(value, axis):
    return [value] + [shift_by(value, axis, s) for s in range(1, lax.axis_size(axis))]


def near_pieces(value, axis):
    return shift_by(value, axis, 1), shift_by(value, axis, -1)


def far_pieces(value, near, axis):
    size = lax.axis_size(axis)
    pieces = [value] + [None] * (size - 1)
    pieces[1], pieces[size - 1] = near
    for s in range(2, size // 2 + 1):
        pieces[s] = shift_by(pieces[s - 1], axis, 1)
    for s in range(2, (size - 1) // 2 + 1):
        pieces[size - s] = shift_by(pieces[size - s + 1], axis, -1)
    return pieces


def phase(*values):
    return lax.optimization_barrier(values)


def after(value, *earlier):
    return lax.optimization_barrier((value, earlier))[0]


def in_order(pieces, axis, dim):
    size, index = len(pieces), lax.axis_index(axis)
    if size == 2:
        first = index == 0
        return jnp.stack(
            [jnp.where(first, pieces[0], pieces[1]), jnp.where(first, pieces[1], pieces[0])], axis=dim
        )
    return jnp.stack(
        [lax.select_n((index - j) % size, *pieces) for j in range(size)], axis=dim
    )


def parted(terms, axis, dim):
    size, index = lax.axis_size(axis), lax.axis_index(axis)

    def slices(i):
        return [lax.dynamic_index_in_dim(t, i, dim, keepdims=False) for t in terms]

    return slices(index) + [
        shift_by(joined(slices((index - s) % size)).astype(BF16), axis, -s) for s in range(1, size)
    ]


def joined(terms):
    total = terms[0].astype(F32)
    for value in terms[1:]:
        total = total + value.astype(F32)
    return total


def columns_home(terms):
    count = lax.axis_size("z")
    local = terms[0].shape[1] // count

    def columns(s):
        return joined([t[:, s * local : (s + 1) * local] for t in terms])

    return [columns(0)] + [shift_by(columns(s).astype(BF16), "z", -s) for s in range(1, count)]


def home(block):
    count, size = lax.axis_size("z"), lax.axis_size("b")
    moves = []
    for t in range(count):
        for z in range(count):
            team = (z % size) * 2 + z // size
            moves.append((team * count + t, t * count + z))
    return lax.ppermute(block, ("b", "c", "z"), moves)


def partner(value, bit):
    count = lax.axis_size(EVERY)
    return lax.ppermute(value, EVERY, [(i, i ^ bit) for i in range(count)])


def exchange_order():
    bits = [1 << i for i in range(lax.axis_size(EVERY).bit_length() - 1)]
    core = lax.axis_size("z")
    return [b for b in bits if b < core] + [b for b in bits[::-1] if b > core] + [core]


def entry_of(difference):
    return sum(((difference & bit) // bit) << i for i, bit in enumerate(exchange_order()))


def told(value, bits):
    for bit in bits:
        value = jnp.concatenate([value, partner(value, bit)], axis=0)
    return value


def first_kernel(steps, *refs):
    near_hidden, far_hidden, w_gate, w_up = refs[:4]
    gates, ups, activated = refs[-3:]
    near = pl.program_id(0) < steps
    hidden = jnp.where(near, near_hidden[...], far_hidden[...])
    gate = dot_nn(hidden, w_gate[...])
    up = dot_nn(hidden, w_up[...])
    gates[...] = gate.astype(BF16)
    ups[...] = up.astype(BF16)
    activated[...] = (gate * (1.0 / (1.0 + jnp.exp(-gate))) * up).astype(BF16)


def second_kernel(steps, *refs):
    near_cot, far_cot, gates, ups, activated, w_gate, w_up, w_down = refs[:8]
    grads, near_back, far_back, near_out, far_out = refs[-5:]
    units = w_down.shape[1]
    near = pl.program_id(0) < steps
    cot = jnp.where(near, near_cot[...], far_cot[...])
    grad = dot_nn(cot, w_down[...])
    gate, up = gates[...].astype(F32), ups[...].astype(F32)
    sigmoid = 1.0 / (1.0 + jnp.exp(-gate))
    to_gate = (grad * up * (sigmoid * (1.0 + gate * (1.0 - sigmoid)))).astype(BF16)
    to_up = (grad * (gate * sigmoid)).astype(BF16)
    grads[:, :units] = to_gate
    grads[:, units:] = to_up
    back = (dot_nt(to_gate, w_gate[...]) + dot_nt(to_up, w_up[...])).astype(BF16)
    out = dot_nt(activated[...], w_down[...]).astype(BF16)

    @pl.when(near)
    def _():
        near_back[...] = back
        near_out[...] = out

    @pl.when(jnp.logical_not(near))
    def _():
        far_back[...] = back
        far_out[...] = out


def feed_forward(second, part, parts, tokens, whole, weights, held):
    rows, width = tokens[0].shape
    units = weights[0].shape[1]
    tile = min(rows, 256)
    steps = rows // tile
    near = pl.BlockSpec((tile, width), lambda i: (jnp.minimum(i, steps - 1), 0))
    far = pl.BlockSpec((tile, width), lambda i: (jnp.maximum(i - steps, 0), 0))
    weight = pl.BlockSpec((width, units), lambda i: (0, 0), pipeline_mode=pl.Buffered(1))

    def of_whole(columns):
        return pl.BlockSpec((tile, columns), lambda i: (part * 2 * steps + i, 0))

    kept = (2 * units,) if second else (units,) * 3
    first_held = 2 + len(whole) + len(weights)
    products = 8 if second else 4
    return pl.pallas_call(
        functools.partial(second_kernel if second else first_kernel, steps),
        grid=(2 * steps,),
        in_specs=[near, far]
        + [of_whole(units)] * len(whole)
        + [weight] * len(weights)
        + [pl.BlockSpec(memory_space=pl.ANY)] * len(held),
        out_specs=[of_whole(n) for n in kept] + ([near, far] * 2 if second else []),
        out_shape=[jax.ShapeDtypeStruct((parts * 2 * rows, n), BF16) for n in kept]
        + [jax.ShapeDtypeStruct((rows, width), BF16)] * (4 if second else 0),
        input_output_aliases={first_held + i: i for i in range(len(held))},
        compiler_params=pltpu.CompilerParams(vmem_limit_bytes=58 * 2**20),
        cost_estimate=pl.CostEstimate(
            flops=2 * products * 2 * rows * width * units,
            bytes_accessed=2 * (2 * rows * width + len(weights) * width * units + 10 * rows * units),
            transcendentals=2 * rows * units,
        ),
        name="second_half" if second else "first_half",
    )(*tokens, *whole, *weights, *held)


def gradient_kernel(*refs, count, extra):
    side, tokens, right, result = refs[0], refs[1 : 1 + count], refs[1 + count], refs[-1]
    del side
    rows = tokens[0].shape[0]
    total = refs[2 + count][...].astype(F32) if extra else None
    for i in range(count):
        term = lax.dot_general(
            tokens[i][...], right[i * rows : (i + 1) * rows, :], (((0,), (0,)), ((), ())), preferred_element_type=F32
        )
        total = term if total is None else total + term
    result[...] = total.astype(BF16)


def gradient_half(side, tokens, right, units, column=0, extra=()):
    rows, width = tokens[0].shape
    count, half = len(tokens), width // 2
    tile = 256 if units % 256 == 0 else 128
    steps = units // tile
    out = pl.BlockSpec((half, tile), lambda j, side: (0, j))
    return pl.pallas_call(
        functools.partial(gradient_kernel, count=count, extra=len(extra)),
        grid_spec=pltpu.PrefetchScalarGridSpec(
            num_scalar_prefetch=1,
            grid=(steps,),
            in_specs=[
                pl.BlockSpec((rows, half), lambda j, side: (0, side[0]), pipeline_mode=pl.Buffered(1))
            ]
            * count
            + [pl.BlockSpec((count * rows, tile), lambda j, side: (0, column * steps + j))]
            + [out] * len(extra),
            out_specs=out,
        ),
        out_shape=jax.ShapeDtypeStruct((half, units), BF16),
        compiler_params=pltpu.CompilerParams(vmem_limit_bytes=40 * 2**20),
        cost_estimate=pl.CostEstimate(
            flops=2 * count * rows * half * units,
            bytes_accessed=2 * (count * rows * (half + units) + half * units),
            transcendentals=0,
        ),
        name="gradient_half",
    )(side.reshape(1).astype(jnp.int32), *tokens, right, *extra)


def split_kernel(core, left, right, kept, leaving):
    total = lax.dot_general(left[...], right[...], (((0,), (0,)), ((), ())), preferred_element_type=F32)
    groups, _, rows, _ = (kept.shape[0], 2, *kept.shape[1:])
    total = total.astype(BF16).reshape(groups, 2, rows, -1)
    first = core[0] == 0
    kept[...] = jnp.where(first, total[:, 0], total[:, 1])
    leaving[...] = jnp.where(first, total[:, 1], total[:, 0])


def split_gradient(core, left, right, groups):
    count, width = left.shape
    columns = right.shape[1]
    tile = 256
    rows = width // (2 * groups)
    out = pl.BlockSpec((groups, rows, tile), lambda j, core: (0, 0, j))
    return pl.pallas_call(
        split_kernel,
        grid_spec=pltpu.PrefetchScalarGridSpec(
            num_scalar_prefetch=1,
            grid=(columns // tile,),
            in_specs=[
                pl.BlockSpec((count, width), lambda j, core: (0, 0), pipeline_mode=pl.Buffered(1)),
                pl.BlockSpec((count, tile), lambda j, core: (0, j)),
            ],
            out_specs=[out, out],
        ),
        out_shape=[jax.ShapeDtypeStruct((groups, rows, columns), BF16)] * 2,
        compiler_params=pltpu.CompilerParams(vmem_limit_bytes=40 * 2**20),
        cost_estimate=pl.CostEstimate(
            flops=2 * count * width * columns,
            bytes_accessed=2 * (count * (width + columns) + width * columns),
            transcendentals=0,
        ),
        name="split_gradient",
    )(core.reshape(1).astype(jnp.int32), left, right)


def per_device(
    tokens,
    lengths,
    permutation,
    cotangent,
    norm1_gain,
    mixer_in,
    mixer_gate,
    conv_kernel,
    mixer_out,
    norm2_gain,
    ffn_gate,
    ffn_up,
    ffn_down,
):
    micro, length, width = tokens.shape
    count_b, count_z = lax.axis_size("b"), lax.axis_size("z")
    ia, ib, ic, iz = (lax.axis_index(n) for n in EVERY)
    place = ((ia * count_b + ib) * 2 + ic) * count_z + iz
    per_block = BLOCK // length
    blocks = permutation.shape[1]
    local = conv_kernel.shape[1]
    rows = micro * length

    dealt = lax.dynamic_slice_in_dim(permutation, place // per_block, 1, axis=1)[:, 0]
    own = dealt * per_block + place % per_block
    spots = jnp.arange(blocks, dtype=jnp.int32)

    def holder(piece):
        at = jnp.sum(jnp.where(permutation == (piece // per_block)[:, None], spots[None, :], 0), axis=1)
        return at * per_block + piece % per_block

    before = holder(jnp.maximum(own - 1, 0))
    last = blocks * per_block - 1
    behind = holder(jnp.minimum(own + 1, last))
    order = jnp.arange(lengths.shape[1], dtype=jnp.int32)
    offsets = jnp.sum(jnp.where(order[None, None, :] < order[None, :, None], lengths[:, None, :], 0), axis=2)
    position = own[:, None] * length + jnp.arange(length, dtype=jnp.int32)[None, :]
    is_start = jnp.any(position[:, :, None] == offsets[:, None, :], axis=2)
    was_start = jnp.any(position[:, :, None] - 1 == offsets[:, None, :], axis=2)
    keep_one = jnp.where(is_start, 0.0, 1.0).astype(F32)[:, :, None]
    keep_two = jnp.where(is_start | was_start, 0.0, 1.0).astype(F32)[:, :, None]

    units = -(-ffn_gate.shape[1] // 128) * 128
    spare = ((0, 0), (0, units - ffn_gate.shape[1]))

    def rows_of(pieces):
        return lax.all_gather(jnp.concatenate(pieces, axis=1), ("a", "b", "c"), axis=0, tiled=True)

    def told_at_once(value):
        return lax.all_gather(lax.all_gather(value, "z", axis=0), ("a", "b", "c"), axis=0)

    def in_plane(value):
        value = value.reshape(2, count_b, *value.shape[1:])
        mine = lax.dynamic_index_in_dim(value, ic, 0, keepdims=False)
        far = shift_by(lax.dynamic_index_in_dim(value, 1 - ic, 0, keepdims=False), "c", 1)
        value = in_order([mine, far], "c", 1)
        pieces = [lax.dynamic_index_in_dim(value, ib, 0, keepdims=False)]
        for s in range(1, count_b):
            leaving = lax.dynamic_index_in_dim(value, (ib + s) % count_b, 0, keepdims=False)
            pieces.append(shift_by(leaving, "b", s))
        return pieces

    def plane_rows(pieces):
        value = in_order(pieces, "b", 0)
        return value.reshape(-1, *value.shape[2:])

    bits = exchange_order()
    tap_count = conv_kernel.size
    told_rows = jnp.concatenate(
        [
            tokens[:, length - 2 :, :].reshape(micro * 2, width).astype(F32),
            jnp.pad(conv_kernel.reshape(1, tap_count), ((0, 0), (0, width - tap_count))),
        ]
    )[None]
    pad_g, pad_u, pad_d = (jnp.pad(w, spare) for w in (ffn_gate, ffn_up, ffn_down))
    z_in = pieces_of(mixer_in, "z")
    told_rows = told(told_rows, bits[:-3])
    far_cotangent = pieces_of(cotangent.reshape(rows, width), "b")
    z_in, told_rows, far_cotangent, mixer_gate, mixer_out, pad_g = phase(
        z_in, told_rows, far_cotangent, mixer_gate, mixer_out, pad_g
    )
    w_in = rows_of(z_in)
    z_gate = pieces_of(mixer_gate, "z")
    near_g = near_pieces(pad_g, "z")
    z_gate, near_g, told_rows, mixer_out, pad_u, pad_d = phase(z_gate, near_g, told_rows, mixer_out, pad_u, pad_d)
    w_gate = rows_of(z_gate)
    z_out = pieces_of(mixer_out, "z")
    z_g = far_pieces(pad_g, near_g, "z")
    told_rows = told(told_rows, bits[-3:-2])
    z_out, z_g, told_rows, pad_u, pad_d, w_in = phase(z_out, z_g, told_rows, pad_u, pad_d, w_in)
    w_out = rows_of(z_out)
    plane_g = in_plane(in_order(z_g, "z", 0))
    z_u = pieces_of(pad_u, "z")
    told_rows = told(told_rows, bits[-2:])
    plane_g, z_u, told_rows, pad_d, w_gate = phase(plane_g, z_u, told_rows, pad_d, w_gate)
    y_g = pieces_of(plane_rows(plane_g), "a")
    plane_u = in_plane(in_order(z_u, "z", 0))
    z_d = pieces_of(pad_d, "z")
    kernel = jnp.concatenate(
        [
            lax.dynamic_slice(
                told_rows, (entry_of(place ^ (place - iz + (iz - s) % count_z)), micro * 2, 0), (1, 1, tap_count)
            ).reshape(3, local)
            for s in range(count_z)
        ],
        axis=1,
    )
    y_g, plane_u, z_d, w_out = phase(y_g, plane_u, z_d, w_out)
    y_u = pieces_of(plane_rows(plane_u), "a")
    plane_d = in_plane(in_order(z_d, "z", 0))
    ffn_g = in_order(y_g, "a", 0).reshape(-1, units)

    tail_in = jnp.concatenate(
        [
            lax.dynamic_slice(told_rows, (entry_of(before[m] ^ place), 2 * m, 0), (1, 2, width))[0]
            for m in range(micro)
        ]
    )
    local_in = tokens.reshape(rows, width).astype(F32)
    local_cot = cotangent.reshape(rows, width).astype(F32)
    scale_one = lax.rsqrt(jnp.mean(local_in * local_in, axis=1, keepdims=True) + EPSILON)
    normed_one = local_in * scale_one
    hidden_one = (normed_one * norm1_gain).astype(BF16)
    tail_scale = lax.rsqrt(jnp.mean(tail_in * tail_in, axis=1, keepdims=True) + EPSILON)
    tail_hidden = (tail_in * tail_scale * norm1_gain).astype(BF16)
    channels = kernel.shape[1]
    signal = dot_nn(hidden_one, w_in).reshape(micro, length, channels)
    tail_signal = dot_nn(tail_hidden, w_in).reshape(micro, 2, channels)
    gating = dot_nn(hidden_one, w_gate).reshape(micro, length, channels)
    extended = jnp.concatenate([tail_signal, signal], axis=1)
    shift_one = keep_one * extended[:, 1 : length + 1, :]
    shift_two = keep_two * extended[:, 0:length, :]
    mixed = kernel[0] * signal + kernel[1] * shift_one + kernel[2] * shift_two
    product = (mixed * gating).astype(BF16).reshape(rows, channels)
    residual = local_in + dot_nt(product, w_out)

    scale_two = lax.rsqrt(jnp.mean(residual * residual, axis=1, keepdims=True) + EPSILON)
    normed_two = residual * scale_two
    hidden_own = (normed_two * norm2_gain).astype(BF16)


    def with_core(pieces):
        return [v for piece in pieces for v in (piece, shift_by(piece, "c", 1))]

    plane_d, y_u, ffn_g, hidden_own = phase(plane_d, y_u, ffn_g, hidden_own)
    y_d = pieces_of(plane_rows(plane_d), "a")
    ffn_u = in_order(y_u, "a", 0).reshape(-1, units)
    far_hidden = pieces_of(hidden_own, "b")[1:]
    hidden_parts = with_core([hidden_own])
    kept = feed_forward(False, 0, count_b, hidden_parts, (), (ffn_g, ffn_u), ())
    y_d, far_hidden, kept = phase(y_d, far_hidden, kept)
    hidden_parts = hidden_parts + with_core(far_hidden)
    for s in range(1, count_b):
        kept = feed_forward(False, s, count_b, hidden_parts[2 * s : 2 * s + 2], (), (ffn_g, ffn_u), kept)
    gates, ups, activated = kept
    ffn_d = in_order(y_d, "a", 0).reshape(-1, units)
    cot_parts = with_core(far_cotangent)
    other = 1 - ia
    leaving_down = gradient_half(other, cot_parts, activated, units)
    leaving_down, cot_parts, hidden_parts = phase(leaving_down, cot_parts, hidden_parts)
    come_down = shift_by(leaving_down, "a", 1)
    held, backs, outs = (), [], []
    for s in range(count_b):
        pair = cot_parts[2 * s : 2 * s + 2]
        *held, near_back, far_back, near_out, far_out = feed_forward(
            True, s, count_b, pair, (gates, ups, activated), (ffn_g, ffn_u, ffn_d), held
        )
        backs.append((near_back, shift_by(far_back, "c", 1)))
        outs.append((near_out, shift_by(far_out, "c", 1)))
    grads = held[0]

    def to_owners(sums):
        return [(near.astype(F32) + far.astype(F32)).astype(BF16) for near, far in sums[1:]]

    def passed(values):
        return [shift_by(v, "b", -1 - i) for i, v in enumerate(values)]

    def over_z(stay, come):
        return lax.psum_scatter(joined([stay, come]).astype(BF16), "z", scatter_dimension=0, tiled=True)

    leaving_gate = gradient_half(other, hidden_parts, grads, units)
    leaving_gate, come_down, backs, outs, hidden_parts, cot_parts = phase(
        leaving_gate, come_down, backs, outs, hidden_parts, cot_parts
    )
    come_gate, came_back = shift_by(leaving_gate, "a", 1), passed(to_owners(backs))
    leaving_up = gradient_half(other, hidden_parts, grads, units, 1)
    stay_down = gradient_half(ia, cot_parts, activated, units)
    stay_gate = gradient_half(ia, hidden_parts, grads, units)
    stay_up = gradient_half(ia, hidden_parts, grads, units, 1)
    leaving_out = to_owners(outs)
    come_gate, came_back, leaving_up, stay_down, stay_gate, stay_up, outs, leaving_out = phase(
        come_gate, came_back, leaving_up, stay_down, stay_gate, stay_up, outs, leaving_out
    )
    come_up, came_out = shift_by(leaving_up, "a", 1), passed(leaving_out)
    scattered_down = over_z(stay_down, come_down)
    grad_hidden_two = joined([*backs[0], *came_back])

    grad_gain_two = jnp.sum(grad_hidden_two * normed_two, axis=0)
    grad_norm_two = grad_hidden_two * norm2_gain
    inner_two = jnp.mean(grad_norm_two * normed_two, axis=1, keepdims=True)
    grad_residual = local_cot + scale_two * (grad_norm_two - normed_two * inner_two)
    grad_branch = grad_residual.astype(BF16)
    grad_product = dot_nn(grad_branch, w_out).reshape(micro, length, channels)
    def over_c(split):
        kept, leaving = split
        shape = (2, count_b, *kept.shape[1:])
        return [kept.reshape(shape), shift_by(leaving, "c", 1).reshape(shape)]

    def split(left, right):
        return split_gradient(ic, left, right, 2 * count_b)

    out_split = split(grad_branch, product)
    grad_mixed = grad_product * gating
    grad_gating = (grad_product * mixed).astype(BF16).reshape(rows, channels)
    grad_kernel = jnp.stack(
        [
            jnp.sum(grad_mixed * signal, axis=(0, 1)),
            jnp.sum(grad_mixed * shift_one, axis=(0, 1)),
            jnp.sum(grad_mixed * shift_two, axis=(0, 1)),
        ]
    )
    into_one = kernel[1] * (keep_one * grad_mixed)
    into_two = kernel[2] * (keep_two * grad_mixed)
    leaving = jnp.stack([into_two[:, 0], into_one[:, 0] + into_two[:, 1]], axis=1)
    blocked = leaving.reshape(micro, 2, count_z, local)

    def turned(value, dim):
        picks = [
            lax.dynamic_index_in_dim(value, (iz - j) % count_z, dim, keepdims=False) for j in range(count_z)
        ]
        return jnp.concatenate(picks, axis=-1)

    blocked = turned(blocked, 2).reshape(micro * 2, channels).astype(BF16)
    gate_split = split(hidden_one, grad_gating)
    from_gating = dot_nt(grad_gating, w_gate)
    blocked, come_up, came_out, out_split, gate_split, grad_mixed, from_gating = phase(
        blocked, come_up, came_out, out_split, gate_split, grad_mixed, from_gating
    )
    everyone = told_at_once(blocked)
    scattered_gate = over_z(stay_gate, come_gate)
    out_c, gate_c = over_c(out_split), over_c(gate_split)
    everyone, out_c, gate_c, grad_mixed, scattered_down = phase(everyone, out_c, gate_c, grad_mixed, scattered_down)
    out_b = parted(out_c, "b", 1)
    gate_a = parted(gate_c, "a", 0)
    down_home = home(scattered_down)
    scattered_up = over_z(stay_up, come_up)
    into_one = kernel[1] * (keep_one * grad_mixed)
    into_two = kernel[2] * (keep_two * grad_mixed)
    arrived = jnp.stack(
        [
            lax.dynamic_slice(
                everyone, (behind[m] // count_z, behind[m] % count_z, 2 * m, 0), (1, 1, 2, channels)
            )[0, 0]
            for m in range(micro)
        ]
    )
    arrived = turned(arrived.reshape(micro, 2, count_z, local), 2).astype(F32)
    arrived = jnp.where((own == last)[:, None, None], 0.0, arrived)
    from_one = jnp.concatenate([into_one[:, 1:], arrived[:, 1:]], axis=1)
    from_two = jnp.concatenate([into_two[:, 2:], arrived[:, :1], jnp.zeros_like(arrived[:, :1])], axis=1)
    grad_signal = (kernel[0] * grad_mixed + from_one + from_two).astype(BF16).reshape(rows, channels)
    in_split = split(hidden_one, grad_signal)
    grad_hidden_one = dot_nt(grad_signal, w_in) + from_gating
    grad_gain_one = jnp.sum(grad_hidden_one * normed_one, axis=0)
    grad_norm_one = grad_hidden_one * norm1_gain
    inner_one = jnp.mean(grad_norm_one * normed_one, axis=1, keepdims=True)
    input_grad = grad_residual + scale_one * (grad_norm_one - normed_one * inner_one)
    out_b, gate_a, in_split, input_grad, down_home, grad_gain_one, outs, scattered_gate = phase(
        out_b, gate_a, in_split, input_grad, down_home, grad_gain_one, outs, scattered_gate
    )
    in_c = over_c(in_split)
    middle = channels // 2
    in_a = parted([t[..., :middle] for t in in_c], "a", 0)
    in_b = parted([t[..., middle:] for t in in_c], "b", 1)
    gate_b = parted(gate_a, "b", 0)
    out_a = parted(out_b, "a", 0)
    gate_home = home(scattered_gate)
    output = (joined([*outs[0], *came_out]) + residual).astype(BF16)
    small = jnp.concatenate(
        [grad_gain_one[None], grad_gain_two[None], turned(grad_kernel.reshape(3, count_z, local), 1)]
    )
    small = lax.all_gather(small, EVERY, axis=0)
    in_a, in_b, gate_b, out_a, gate_home, scattered_up, output = phase(
        in_a, in_b, gate_b, out_a, gate_home, scattered_up, output
    )
    in_a, in_b = parted(in_a, "b", 0), parted(in_b, "a", 0)
    up_home = home(scattered_up)
    two_z = columns_home([jnp.concatenate([joined(out_a), joined(gate_b)], axis=0)])
    in_a, in_b, two_z, small, up_home = phase(in_a, in_b, two_z, small, up_home)
    in_z = columns_home([jnp.concatenate([joined(in_a), joined(in_b)], axis=1)])
    share = width // (4 * count_b * count_z)
    gains = lax.dynamic_slice_in_dim(small[:, :2], place * share, share, axis=2)
    tap_grads = lax.dynamic_slice_in_dim(
        small[:, 2:], (iz * 4 * count_b + place // count_z) * share, share, axis=2
    )
    gains, tap_grads = jnp.sum(gains, axis=0), jnp.sum(tap_grads, axis=0)
    grad_out, grad_gate_w = jnp.split(joined(two_z), 2)
    grad_in_w = joined(in_z)
    hidden_units = ffn_gate.shape[1]
    grad_ffg, grad_ffu, grad_down = (g[:, :hidden_units].astype(F32) for g in (gate_home, up_home, down_home))

    return (
        output.reshape(micro, length, width),
        input_grad.reshape(micro, length, width),
        gains[0],
        grad_in_w,
        grad_gate_w,
        tap_grads,
        grad_out,
        gains[1],
        grad_ffg,
        grad_ffu,
        grad_down,
    )


def solution(mesh):
    row, col = mesh.shape["row"], mesh.shape["col"]
    fine = Mesh(mesh.devices.reshape(2, row // 4, 2, col), EVERY)
    by_rows = ("a", "b", "c")
    matrix = P(by_rows, "z")
    token = P(None, EVERY, None)
    return jax.shard_map(
        per_device,
        mesh=fine,
        in_specs=(
            token,
            P(),
            P(),
            token,
            P(),
            matrix,
            matrix,
            P(None, "z"),
            matrix,
            P(),
            matrix,
            matrix,
            matrix,
        ),
        out_specs=(
            token,
            token,
            P(EVERY),
            matrix,
            matrix,
            P(None, ("z", *by_rows)),
            matrix,
            P(EVERY),
            matrix,
            matrix,
            matrix,
        ),
        check_vma=False,
    )
```

```python
import functools

import jax
import jax.numpy as jnp
from jax import lax
from jax.experimental import pallas as pl
from jax.experimental.pallas import tpu as pltpu
from jax.sharding import Mesh
from jax.sharding import PartitionSpec as P

BLOCK = 128
EPSILON = 1e-05
F32 = jnp.float32
BF16 = jnp.bfloat16
EVERY = ("a", "b", "c", "z")


def dot_nn(left, right):
    return lax.dot_general(left, right, (((1,), (0,)), ((), ())), preferred_element_type=F32)


def dot_nt(left, right):
    return lax.dot_general(left, right, (((1,), (1,)), ((), ())), preferred_element_type=F32)


def dot_tn(left, right):
    return lax.dot_general(left, right, (((0,), (0,)), ((), ())), preferred_element_type=F32)


def shift_by(value, axis, amount):
    size = lax.axis_size(axis)
    return lax.ppermute(value, axis, [(i, (i + amount) % size) for i in range(size)])


def pieces_of(value, axis):
    return [value] + [shift_by(value, axis, s) for s in range(1, lax.axis_size(axis))]


def near_pieces(value, axis):
    return shift_by(value, axis, 1), shift_by(value, axis, -1)


def far_pieces(value, near, axis):
    size = lax.axis_size(axis)
    pieces = [value] + [None] * (size - 1)
    pieces[1], pieces[size - 1] = near
    for s in range(2, size // 2 + 1):
        pieces[s] = shift_by(pieces[s - 1], axis, 1)
    for s in range(2, (size - 1) // 2 + 1):
        pieces[size - s] = shift_by(pieces[size - s + 1], axis, -1)
    return pieces


def phase(*values):
    return lax.optimization_barrier(values)


def after(value, *earlier):
    return lax.optimization_barrier((value, earlier))[0]


def in_order(pieces, axis, dim):
    size, index = len(pieces), lax.axis_index(axis)
    if size == 2:
        first = index == 0
        return jnp.stack(
            [jnp.where(first, pieces[0], pieces[1]), jnp.where(first, pieces[1], pieces[0])], axis=dim
        )
    return jnp.stack(
        [lax.select_n((index - j) % size, *pieces) for j in range(size)], axis=dim
    )


def parted(terms, axis, dim):
    size, index = lax.axis_size(axis), lax.axis_index(axis)

    def slices(i):
        return [lax.dynamic_index_in_dim(t, i, dim, keepdims=False) for t in terms]

    return slices(index) + [
        shift_by(joined(slices((index - s) % size)).astype(BF16), axis, -s) for s in range(1, size)
    ]


def joined(terms):
    total = terms[0].astype(F32)
    for value in terms[1:]:
        total = total + value.astype(F32)
    return total


def columns_home(terms):
    count = lax.axis_size("z")
    local = terms[0].shape[1] // count

    def columns(s):
        return joined([t[:, s * local : (s + 1) * local] for t in terms])

    return [columns(0)] + [shift_by(columns(s).astype(BF16), "z", -s) for s in range(1, count)]


def home(block):
    count, size = lax.axis_size("z"), lax.axis_size("b")
    moves = []
    for t in range(count):
        for z in range(count):
            team = (z % size) * 2 + z // size
            moves.append((team * count + t, t * count + z))
    return lax.ppermute(block, ("b", "c", "z"), moves)


def partner(value, bit):
    count = lax.axis_size(EVERY)
    return lax.ppermute(value, EVERY, [(i, i ^ bit) for i in range(count)])


def exchange_order():
    bits = [1 << i for i in range(lax.axis_size(EVERY).bit_length() - 1)]
    core = lax.axis_size("z")
    return [b for b in bits if b < core] + [b for b in bits[::-1] if b > core] + [core]


def entry_of(difference):
    return sum(((difference & bit) // bit) << i for i, bit in enumerate(exchange_order()))


def told(value, bits):
    for bit in bits:
        value = jnp.concatenate([value, partner(value, bit)], axis=0)
    return value


def first_kernel(steps, *refs):
    near_hidden, far_hidden, w_gate, w_up = refs[:4]
    gates, ups, activated = refs[-3:]
    near = pl.program_id(0) < steps
    hidden = jnp.where(near, near_hidden[...], far_hidden[...])
    gate = dot_nn(hidden, w_gate[...])
    up = dot_nn(hidden, w_up[...])
    gates[...] = gate.astype(BF16)
    ups[...] = up.astype(BF16)
    activated[...] = (gate * (1.0 / (1.0 + jnp.exp(-gate))) * up).astype(BF16)


def second_kernel(steps, *refs):
    near_cot, far_cot, gates, ups, activated, w_gate, w_up, w_down = refs[:8]
    grads, near_back, far_back, near_out, far_out = refs[-5:]
    units = w_down.shape[1]
    near = pl.program_id(0) < steps
    cot = jnp.where(near, near_cot[...], far_cot[...])
    grad = dot_nn(cot, w_down[...])
    gate, up = gates[...].astype(F32), ups[...].astype(F32)
    sigmoid = 1.0 / (1.0 + jnp.exp(-gate))
    to_gate = (grad * up * (sigmoid * (1.0 + gate * (1.0 - sigmoid)))).astype(BF16)
    to_up = (grad * (gate * sigmoid)).astype(BF16)
    grads[:, :units] = to_gate
    grads[:, units:] = to_up
    back = (dot_nt(to_gate, w_gate[...]) + dot_nt(to_up, w_up[...])).astype(BF16)
    out = dot_nt(activated[...], w_down[...]).astype(BF16)

    @pl.when(near)
    def _():
        near_back[...] = back
        near_out[...] = out

    @pl.when(jnp.logical_not(near))
    def _():
        far_back[...] = back
        far_out[...] = out


def feed_forward(second, part, parts, tokens, whole, weights, held):
    rows, width = tokens[0].shape
    units = weights[0].shape[1]
    tile = min(rows, 256)
    steps = rows // tile
    near = pl.BlockSpec((tile, width), lambda i: (jnp.minimum(i, steps - 1), 0))
    far = pl.BlockSpec((tile, width), lambda i: (jnp.maximum(i - steps, 0), 0))
    weight = pl.BlockSpec((width, units), lambda i: (0, 0), pipeline_mode=pl.Buffered(1))

    def of_whole(columns):
        return pl.BlockSpec((tile, columns), lambda i: (part * 2 * steps + i, 0))

    kept = (2 * units,) if second else (units,) * 3
    first_held = 2 + len(whole) + len(weights)
    products = 8 if second else 4
    return pl.pallas_call(
        functools.partial(second_kernel if second else first_kernel, steps),
        grid=(2 * steps,),
        in_specs=[near, far]
        + [of_whole(units)] * len(whole)
        + [weight] * len(weights)
        + [pl.BlockSpec(memory_space=pl.ANY)] * len(held),
        out_specs=[of_whole(n) for n in kept] + ([near, far] * 2 if second else []),
        out_shape=[jax.ShapeDtypeStruct((parts * 2 * rows, n), BF16) for n in kept]
        + [jax.ShapeDtypeStruct((rows, width), BF16)] * (4 if second else 0),
        input_output_aliases={first_held + i: i for i in range(len(held))},
        compiler_params=pltpu.CompilerParams(vmem_limit_bytes=58 * 2**20),
        cost_estimate=pl.CostEstimate(
            flops=2 * products * 2 * rows * width * units,
            bytes_accessed=2 * (2 * rows * width + len(weights) * width * units + 10 * rows * units),
            transcendentals=2 * rows * units,
        ),
        name="second_half" if second else "first_half",
    )(*tokens, *whole, *weights, *held)


def gradient_kernel(*refs, count, extra):
    side, tokens, right, result = refs[0], refs[1 : 1 + count], refs[1 + count], refs[-1]
    del side
    rows = tokens[0].shape[0]
    total = refs[2 + count][...].astype(F32) if extra else None
    for i in range(count):
        term = lax.dot_general(
            tokens[i][...], right[i * rows : (i + 1) * rows, :], (((0,), (0,)), ((), ())), preferred_element_type=F32
        )
        total = term if total is None else total + term
    result[...] = total.astype(BF16)


def gradient_half(side, tokens, right, units, column=0, extra=()):
    rows, width = tokens[0].shape
    count, half = len(tokens), width // 2
    tile = 256 if units % 256 == 0 else 128
    steps = units // tile
    out = pl.BlockSpec((half, tile), lambda j, side: (0, j))
    return pl.pallas_call(
        functools.partial(gradient_kernel, count=count, extra=len(extra)),
        grid_spec=pltpu.PrefetchScalarGridSpec(
            num_scalar_prefetch=1,
            grid=(steps,),
            in_specs=[
                pl.BlockSpec((rows, half), lambda j, side: (0, side[0]), pipeline_mode=pl.Buffered(1))
            ]
            * count
            + [pl.BlockSpec((count * rows, tile), lambda j, side: (0, column * steps + j))]
            + [out] * len(extra),
            out_specs=out,
        ),
        out_shape=jax.ShapeDtypeStruct((half, units), BF16),
        compiler_params=pltpu.CompilerParams(vmem_limit_bytes=40 * 2**20),
        cost_estimate=pl.CostEstimate(
            flops=2 * count * rows * half * units,
            bytes_accessed=2 * (count * rows * (half + units) + half * units),
            transcendentals=0,
        ),
        name="gradient_half",
    )(side.reshape(1).astype(jnp.int32), *tokens, right, *extra)


def split_kernel(core, left, right, kept, leaving):
    total = lax.dot_general(left[...], right[...], (((0,), (0,)), ((), ())), preferred_element_type=F32)
    groups, _, rows, _ = (kept.shape[0], 2, *kept.shape[1:])
    total = total.astype(BF16).reshape(groups, 2, rows, -1)
    first = core[0] == 0
    kept[...] = jnp.where(first, total[:, 0], total[:, 1])
    leaving[...] = jnp.where(first, total[:, 1], total[:, 0])


def split_gradient(core, left, right, groups):
    count, width = left.shape
    columns = right.shape[1]
    tile = 256
    rows = width // (2 * groups)
    out = pl.BlockSpec((groups, rows, tile), lambda j, core: (0, 0, j))
    return pl.pallas_call(
        split_kernel,
        grid_spec=pltpu.PrefetchScalarGridSpec(
            num_scalar_prefetch=1,
            grid=(columns // tile,),
            in_specs=[
                pl.BlockSpec((count, width), lambda j, core: (0, 0), pipeline_mode=pl.Buffered(1)),
                pl.BlockSpec((count, tile), lambda j, core: (0, j)),
            ],
            out_specs=[out, out],
        ),
        out_shape=[jax.ShapeDtypeStruct((groups, rows, columns), BF16)] * 2,
        compiler_params=pltpu.CompilerParams(vmem_limit_bytes=40 * 2**20),
        cost_estimate=pl.CostEstimate(
            flops=2 * count * width * columns,
            bytes_accessed=2 * (count * (width + columns) + width * columns),
            transcendentals=0,
        ),
        name="split_gradient",
    )(core.reshape(1).astype(jnp.int32), left, right)


def per_device(
    tokens,
    lengths,
    permutation,
    cotangent,
    norm1_gain,
    mixer_in,
    mixer_gate,
    conv_kernel,
    mixer_out,
    norm2_gain,
    ffn_gate,
    ffn_up,
    ffn_down,
):
    micro, length, width = tokens.shape
    count_b, count_z = lax.axis_size("b"), lax.axis_size("z")
    ia, ib, ic, iz = (lax.axis_index(n) for n in EVERY)
    place = ((ia * count_b + ib) * 2 + ic) * count_z + iz
    per_block = BLOCK // length
    blocks = permutation.shape[1]
    local = conv_kernel.shape[1]
    rows = micro * length

    dealt = lax.dynamic_slice_in_dim(permutation, place // per_block, 1, axis=1)[:, 0]
    own = dealt * per_block + place % per_block
    spots = jnp.arange(blocks, dtype=jnp.int32)

    def holder(piece):
        at = jnp.sum(jnp.where(permutation == (piece // per_block)[:, None], spots[None, :], 0), axis=1)
        return at * per_block + piece % per_block

    before = holder(jnp.maximum(own - 1, 0))
    last = blocks * per_block - 1
    behind = holder(jnp.minimum(own + 1, last))
    order = jnp.arange(lengths.shape[1], dtype=jnp.int32)
    offsets = jnp.sum(jnp.where(order[None, None, :] < order[None, :, None], lengths[:, None, :], 0), axis=2)
    position = own[:, None] * length + jnp.arange(length, dtype=jnp.int32)[None, :]
    is_start = jnp.any(position[:, :, None] == offsets[:, None, :], axis=2)
    was_start = jnp.any(position[:, :, None] - 1 == offsets[:, None, :], axis=2)
    keep_one = jnp.where(is_start, 0.0, 1.0).astype(F32)[:, :, None]
    keep_two = jnp.where(is_start | was_start, 0.0, 1.0).astype(F32)[:, :, None]

    units = -(-ffn_gate.shape[1] // 128) * 128
    spare = ((0, 0), (0, units - ffn_gate.shape[1]))

    def rows_of(pieces):
        return lax.all_gather(jnp.concatenate(pieces, axis=1), ("a", "b", "c"), axis=0, tiled=True)

    def told_at_once(value):
        return lax.all_gather(lax.all_gather(value, "z", axis=0), ("a", "b", "c"), axis=0)

    def in_plane(value):
        value = value.reshape(2, count_b, *value.shape[1:])
        mine = lax.dynamic_index_in_dim(value, ic, 0, keepdims=False)
        far = shift_by(lax.dynamic_index_in_dim(value, 1 - ic, 0, keepdims=False), "c", 1)
        value = in_order([mine, far], "c", 1)
        pieces = [lax.dynamic_index_in_dim(value, ib, 0, keepdims=False)]
        for s in range(1, count_b):
            leaving = lax.dynamic_index_in_dim(value, (ib + s) % count_b, 0, keepdims=False)
            pieces.append(shift_by(leaving, "b", s))
        return pieces

    def plane_rows(pieces):
        value = in_order(pieces, "b", 0)
        return value.reshape(-1, *value.shape[2:])

    bits = exchange_order()
    tap_count = conv_kernel.size
    told_rows = jnp.concatenate(
        [
            tokens[:, length - 2 :, :].reshape(micro * 2, width).astype(F32),
            jnp.pad(conv_kernel.reshape(1, tap_count), ((0, 0), (0, width - tap_count))),
        ]
    )[None]
    pad_g, pad_u, pad_d = (jnp.pad(w, spare) for w in (ffn_gate, ffn_up, ffn_down))
    z_in = pieces_of(mixer_in, "z")
    told_rows = told(told_rows, bits[:-3])
    far_cotangent = pieces_of(cotangent.reshape(rows, width), "b")
    before_at = [entry_of(before[m] ^ place) for m in range(micro)]
    behind_at = [(behind[m] // count_z, behind[m] % count_z) for m in range(micro)]
    z_in, told_rows, far_cotangent, mixer_gate, mixer_out, pad_g, before_at, behind_at = phase(
        z_in, told_rows, far_cotangent, mixer_gate, mixer_out, pad_g, before_at, behind_at
    )
    w_in = rows_of(z_in)
    z_gate = pieces_of(mixer_gate, "z")
    near_g = near_pieces(pad_g, "z")
    z_gate, near_g, told_rows, mixer_out, pad_u, pad_d = phase(z_gate, near_g, told_rows, mixer_out, pad_u, pad_d)
    w_gate = rows_of(z_gate)
    z_out = pieces_of(mixer_out, "z")
    z_g = far_pieces(pad_g, near_g, "z")
    told_rows = told(told_rows, bits[-3:-2])
    z_out, z_g, told_rows, pad_u, pad_d, w_in = phase(z_out, z_g, told_rows, pad_u, pad_d, w_in)
    w_out = rows_of(z_out)
    plane_g = in_plane(in_order(z_g, "z", 0))
    z_u = pieces_of(pad_u, "z")
    told_rows = told(told_rows, bits[-2:])
    plane_g, z_u, told_rows, pad_d, w_gate = phase(plane_g, z_u, told_rows, pad_d, w_gate)
    y_g = pieces_of(plane_rows(plane_g), "a")
    plane_u = in_plane(in_order(z_u, "z", 0))
    z_d = pieces_of(pad_d, "z")
    kernel = jnp.concatenate(
        [
            lax.dynamic_slice(
                told_rows, (entry_of(place ^ (place - iz + (iz - s) % count_z)), micro * 2, 0), (1, 1, tap_count)
            ).reshape(3, local)
            for s in range(count_z)
        ],
        axis=1,
    )
    y_g, plane_u, z_d, w_out = phase(y_g, plane_u, z_d, w_out)
    y_u = pieces_of(plane_rows(plane_u), "a")
    plane_d = in_plane(in_order(z_d, "z", 0))
    ffn_g = in_order(y_g, "a", 0).reshape(-1, units)

    tail_in = jnp.concatenate(
        [
            lax.dynamic_slice(told_rows, (before_at[m], 2 * m, 0), (1, 2, width))[0]
            for m in range(micro)
        ]
    )
    local_in = tokens.reshape(rows, width).astype(F32)
    local_cot = cotangent.reshape(rows, width).astype(F32)
    scale_one = lax.rsqrt(jnp.mean(local_in * local_in, axis=1, keepdims=True) + EPSILON)
    normed_one = local_in * scale_one
    hidden_one = (normed_one * norm1_gain).astype(BF16)
    tail_scale = lax.rsqrt(jnp.mean(tail_in * tail_in, axis=1, keepdims=True) + EPSILON)
    tail_hidden = (tail_in * tail_scale * norm1_gain).astype(BF16)
    channels = kernel.shape[1]
    signal = dot_nn(hidden_one, w_in).reshape(micro, length, channels)
    tail_signal = dot_nn(tail_hidden, w_in).reshape(micro, 2, channels)
    gating = dot_nn(hidden_one, w_gate).reshape(micro, length, channels)
    extended = jnp.concatenate([tail_signal, signal], axis=1)
    shift_one = keep_one * extended[:, 1 : length + 1, :]
    shift_two = keep_two * extended[:, 0:length, :]
    mixed = kernel[0] * signal + kernel[1] * shift_one + kernel[2] * shift_two
    product = (mixed * gating).astype(BF16).reshape(rows, channels)
    residual = local_in + dot_nt(product, w_out)

    scale_two = lax.rsqrt(jnp.mean(residual * residual, axis=1, keepdims=True) + EPSILON)
    normed_two = residual * scale_two
    hidden_own = (normed_two * norm2_gain).astype(BF16)


    def with_core(pieces):
        return [v for piece in pieces for v in (piece, shift_by(piece, "c", 1))]

    plane_d, y_u, ffn_g, hidden_own = phase(plane_d, y_u, ffn_g, hidden_own)
    y_d = pieces_of(plane_rows(plane_d), "a")
    ffn_u = in_order(y_u, "a", 0).reshape(-1, units)
    far_hidden = pieces_of(hidden_own, "b")[1:]
    hidden_parts = with_core([hidden_own])
    kept = feed_forward(False, 0, count_b, hidden_parts, (), (ffn_g, ffn_u), ())
    y_d, far_hidden, kept = phase(y_d, far_hidden, kept)
    hidden_parts = hidden_parts + with_core(far_hidden)
    for s in range(1, count_b):
        kept = feed_forward(False, s, count_b, hidden_parts[2 * s : 2 * s + 2], (), (ffn_g, ffn_u), kept)
    gates, ups, activated = kept
    ffn_d = in_order(y_d, "a", 0).reshape(-1, units)
    cot_parts = with_core(far_cotangent)
    other = 1 - ia
    leaving_down = gradient_half(other, cot_parts, activated, units)
    leaving_down, cot_parts, hidden_parts = phase(leaving_down, cot_parts, hidden_parts)
    come_down = shift_by(leaving_down, "a", 1)
    held, backs, outs = (), [None] * count_b, [None] * count_b
    for s in reversed(range(count_b)):
        pair = cot_parts[2 * s : 2 * s + 2]
        *held, near_back, far_back, near_out, far_out = feed_forward(
            True, s, count_b, pair, (gates, ups, activated), (ffn_g, ffn_u, ffn_d), held
        )
        backs[s] = (near_back, shift_by(far_back, "c", 1))
        outs[s] = (near_out, shift_by(far_out, "c", 1))
    grads = held[0]

    def to_owners(sums):
        return [(near.astype(F32) + far.astype(F32)).astype(BF16) for near, far in sums]

    def passed(values):
        return [shift_by(v, "b", -1 - i) for i, v in enumerate(values)]

    def over_z(stay, come):
        return lax.psum_scatter(joined([stay, come]).astype(BF16), "z", scatter_dimension=0, tiled=True)

    leaving_gate = gradient_half(other, hidden_parts, grads, units)
    own_back, own_out = backs[0], outs[0]
    leaving_gate, come_down, far_backs, far_outs, hidden_parts, cot_parts = phase(
        leaving_gate, come_down, backs[1:], outs[1:], hidden_parts, cot_parts
    )
    come_gate, came_back = shift_by(leaving_gate, "a", 1), passed(to_owners(far_backs))
    leaving_up = gradient_half(other, hidden_parts, grads, units, 1)
    stay_down = gradient_half(ia, cot_parts, activated, units)
    stay_gate = gradient_half(ia, hidden_parts, grads, units)
    stay_up = gradient_half(ia, hidden_parts, grads, units, 1)
    leaving_out = to_owners(far_outs)
    scattered_down = over_z(stay_down, come_down)
    come_gate, came_back, leaving_up, stay_gate, stay_up, own_back, own_out, leaving_out = phase(
        come_gate, came_back, leaving_up, stay_gate, stay_up, own_back, own_out, leaving_out
    )
    come_up, came_out = shift_by(leaving_up, "a", 1), passed(leaving_out)
    scattered_gate = over_z(stay_gate, come_gate)
    grad_hidden_two = joined([*own_back, *came_back])

    grad_gain_two = jnp.sum(grad_hidden_two * normed_two, axis=0)
    grad_norm_two = grad_hidden_two * norm2_gain
    inner_two = jnp.mean(grad_norm_two * normed_two, axis=1, keepdims=True)
    grad_residual = local_cot + scale_two * (grad_norm_two - normed_two * inner_two)
    grad_branch = grad_residual.astype(BF16)
    grad_product = dot_nn(grad_branch, w_out).reshape(micro, length, channels)
    def over_c(split):
        kept, leaving = split
        shape = (2, count_b, *kept.shape[1:])
        return [kept.reshape(shape), shift_by(leaving, "c", 1).reshape(shape)]

    def split(left, right):
        return split_gradient(ic, left, right, 2 * count_b)

    out_split = split(grad_branch, product)
    grad_mixed = grad_product * gating
    grad_gating = (grad_product * mixed).astype(BF16).reshape(rows, channels)
    grad_kernel = jnp.stack(
        [
            jnp.sum(grad_mixed * signal, axis=(0, 1)),
            jnp.sum(grad_mixed * shift_one, axis=(0, 1)),
            jnp.sum(grad_mixed * shift_two, axis=(0, 1)),
        ]
    )
    into_one = kernel[1] * (keep_one * grad_mixed)
    into_two = kernel[2] * (keep_two * grad_mixed)
    leaving = jnp.stack([into_two[:, 0], into_one[:, 0] + into_two[:, 1]], axis=1)
    blocked = leaving.reshape(micro, 2, count_z, local)

    def turned(value, dim):
        picks = [
            lax.dynamic_index_in_dim(value, (iz - j) % count_z, dim, keepdims=False) for j in range(count_z)
        ]
        return jnp.concatenate(picks, axis=-1)

    blocked = turned(blocked, 2).reshape(micro * 2, channels).astype(BF16)
    gate_split = split(hidden_one, grad_gating)
    from_gating = dot_nt(grad_gating, w_gate)
    blocked, come_up, came_out, out_split, gate_split, grad_mixed, from_gating, scattered_down = phase(
        blocked, come_up, came_out, out_split, gate_split, grad_mixed, from_gating, scattered_down
    )
    everyone = told_at_once(blocked)
    out_c, gate_c = over_c(out_split), over_c(gate_split)
    everyone, out_c, gate_c, grad_mixed, scattered_gate, scattered_down, come_up = phase(
        everyone, out_c, gate_c, grad_mixed, scattered_gate, scattered_down, come_up
    )
    scattered_up = over_z(stay_up, come_up)
    out_b = parted(out_c, "b", 1)
    gate_a = parted(gate_c, "a", 0)
    down_home = home(scattered_down)
    into_one = kernel[1] * (keep_one * grad_mixed)
    into_two = kernel[2] * (keep_two * grad_mixed)
    arrived = jnp.stack(
        [
            lax.dynamic_slice(
                everyone, (*behind_at[m], 2 * m, 0), (1, 1, 2, channels)
            )[0, 0]
            for m in range(micro)
        ]
    )
    arrived = turned(arrived.reshape(micro, 2, count_z, local), 2).astype(F32)
    arrived = jnp.where((own == last)[:, None, None], 0.0, arrived)
    from_one = jnp.concatenate([into_one[:, 1:], arrived[:, 1:]], axis=1)
    from_two = jnp.concatenate([into_two[:, 2:], arrived[:, :1], jnp.zeros_like(arrived[:, :1])], axis=1)
    grad_signal = (kernel[0] * grad_mixed + from_one + from_two).astype(BF16).reshape(rows, channels)
    in_split = split(hidden_one, grad_signal)
    grad_hidden_one = dot_nt(grad_signal, w_in) + from_gating
    grad_gain_one = jnp.sum(grad_hidden_one * normed_one, axis=0)
    grad_norm_one = grad_hidden_one * norm1_gain
    inner_one = jnp.mean(grad_norm_one * normed_one, axis=1, keepdims=True)
    input_grad = grad_residual + scale_one * (grad_norm_one - normed_one * inner_one)
    out_b, gate_a, in_split, input_grad, down_home, scattered_gate, grad_gain_one, own_out = phase(
        out_b, gate_a, in_split, input_grad, down_home, scattered_gate, grad_gain_one, own_out
    )
    in_c = over_c(in_split)
    middle = channels // 2
    in_a = parted([t[..., :middle] for t in in_c], "a", 0)
    in_b = parted([t[..., middle:] for t in in_c], "b", 1)
    gate_b = parted(gate_a, "b", 0)
    out_a = parted(out_b, "a", 0)
    gate_home, up_home = home(scattered_gate), home(scattered_up)
    output = (joined([*own_out, *came_out]) + residual).astype(BF16)
    small = jnp.concatenate(
        [grad_gain_one[None], grad_gain_two[None], turned(grad_kernel.reshape(3, count_z, local), 1)]
    )
    small = lax.all_gather(small, EVERY, axis=0)
    in_a, in_b, gate_b, out_a, gate_home, up_home, output = phase(
        in_a, in_b, gate_b, out_a, gate_home, up_home, output
    )
    in_a, in_b = parted(in_a, "b", 0), parted(in_b, "a", 0)
    two_z = columns_home([jnp.concatenate([joined(out_a), joined(gate_b)], axis=0)])
    in_a, in_b, two_z, small = phase(in_a, in_b, two_z, small)
    in_z = columns_home([jnp.concatenate([joined(in_a), joined(in_b)], axis=1)])
    share = width // (4 * count_b * count_z)
    gains = lax.dynamic_slice_in_dim(small[:, :2], place * share, share, axis=2)
    tap_grads = lax.dynamic_slice_in_dim(
        small[:, 2:], (iz * 4 * count_b + place // count_z) * share, share, axis=2
    )
    gains, tap_grads = jnp.sum(gains, axis=0), jnp.sum(tap_grads, axis=0)
    grad_out, grad_gate_w = jnp.split(joined(two_z), 2)
    grad_in_w = joined(in_z)
    hidden_units = ffn_gate.shape[1]
    grad_ffg, grad_ffu, grad_down = (g[:, :hidden_units].astype(F32) for g in (gate_home, up_home, down_home))

    return (
        output.reshape(micro, length, width),
        input_grad.reshape(micro, length, width),
        gains[0],
        grad_in_w,
        grad_gate_w,
        tap_grads,
        grad_out,
        gains[1],
        grad_ffg,
        grad_ffu,
        grad_down,
    )


def solution(mesh):
    row, col = mesh.shape["row"], mesh.shape["col"]
    fine = Mesh(mesh.devices.reshape(2, row // 4, 2, col), EVERY)
    by_rows = ("a", "b", "c")
    matrix = P(by_rows, "z")
    token = P(None, EVERY, None)
    return jax.shard_map(
        per_device,
        mesh=fine,
        in_specs=(
            token,
            P(),
            P(),
            token,
            P(),
            matrix,
            matrix,
            P(None, "z"),
            matrix,
            P(),
            matrix,
            matrix,
            matrix,
        ),
        out_specs=(
            token,
            token,
            P(EVERY),
            matrix,
            matrix,
            P(None, ("z", *by_rows)),
            matrix,
            P(EVERY),
            matrix,
            matrix,
            matrix,
        ),
        check_vma=False,
    )
```

```python
import functools

import jax
import jax.numpy as jnp
from jax import lax
from jax.experimental import pallas as pl
from jax.experimental.pallas import tpu as pltpu
from jax.sharding import Mesh
from jax.sharding import PartitionSpec as P

BLOCK = 128
EPSILON = 1e-05
F32 = jnp.float32
BF16 = jnp.bfloat16
EVERY = ("a", "b", "c", "z")


def dot_nn(left, right):
    return lax.dot_general(left, right, (((1,), (0,)), ((), ())), preferred_element_type=F32)


def dot_nt(left, right):
    return lax.dot_general(left, right, (((1,), (1,)), ((), ())), preferred_element_type=F32)


def dot_tn(left, right):
    return lax.dot_general(left, right, (((0,), (0,)), ((), ())), preferred_element_type=F32)


def shift_by(value, axis, amount):
    size = lax.axis_size(axis)
    return lax.ppermute(value, axis, [(i, (i + amount) % size) for i in range(size)])


def pieces_of(value, axis):
    return [value] + [shift_by(value, axis, s) for s in range(1, lax.axis_size(axis))]


def near_pieces(value, axis):
    return shift_by(value, axis, 1), shift_by(value, axis, -1)


def far_pieces(value, near, axis):
    size = lax.axis_size(axis)
    pieces = [value] + [None] * (size - 1)
    pieces[1], pieces[size - 1] = near
    for s in range(2, size // 2 + 1):
        pieces[s] = shift_by(pieces[s - 1], axis, 1)
    for s in range(2, (size - 1) // 2 + 1):
        pieces[size - s] = shift_by(pieces[size - s + 1], axis, -1)
    return pieces


def phase(*values):
    return lax.optimization_barrier(values)


def after(value, *earlier):
    return lax.optimization_barrier((value, earlier))[0]


def in_order(pieces, axis, dim):
    size, index = len(pieces), lax.axis_index(axis)
    if size == 2:
        first = index == 0
        return jnp.stack(
            [jnp.where(first, pieces[0], pieces[1]), jnp.where(first, pieces[1], pieces[0])], axis=dim
        )
    return jnp.stack(
        [lax.select_n((index - j) % size, *pieces) for j in range(size)], axis=dim
    )


def slices_of(terms, i, dim):
    return [lax.dynamic_index_in_dim(t, i, dim, keepdims=False) for t in terms]


def parted(terms, axis, dim, kind=BF16):
    size, index = lax.axis_size(axis), lax.axis_index(axis)
    return terms, [
        shift_by(joined(slices_of(terms, (index - s) % size, dim)).astype(kind), axis, -s) for s in range(1, size)
    ]


def settled(parts, axis, dim):
    terms, arrived = parts
    return slices_of(terms, lax.axis_index(axis), dim) + arrived


def joined(terms):
    total = terms[0].astype(F32)
    for value in terms[1:]:
        total = total + value.astype(F32)
    return total


def columns_home(terms):
    count = lax.axis_size("z")
    local = terms[0].shape[1] // count

    def columns(s):
        return joined([t[:, s * local : (s + 1) * local] for t in terms])

    return [columns(0)] + [shift_by(columns(s).astype(BF16), "z", -s) for s in range(1, count)]


def home(block):
    count, size = lax.axis_size("z"), lax.axis_size("b")
    moves = []
    for t in range(count):
        for z in range(count):
            team = (z % size) * 2 + z // size
            moves.append((team * count + t, t * count + z))
    return lax.ppermute(block, ("b", "c", "z"), moves)


def partner(value, bit):
    count = lax.axis_size(EVERY)
    return lax.ppermute(value, EVERY, [(i, i ^ bit) for i in range(count)])


def exchange_order():
    bits = [1 << i for i in range(lax.axis_size(EVERY).bit_length() - 1)]
    core = lax.axis_size("z")
    return [b for b in bits if b < core] + [b for b in bits[::-1] if b > core] + [core]


def entry_of(difference):
    return sum(((difference & bit) // bit) << i for i, bit in enumerate(exchange_order()))


def told(value, bits):
    for bit in bits:
        value = jnp.concatenate([value, partner(value, bit)], axis=0)
    return value


def first_kernel(steps, *refs):
    near_hidden, far_hidden, w_gate, w_up = refs[:4]
    gates, ups, activated = refs[-3:]
    near = pl.program_id(0) < steps
    hidden = jnp.where(near, near_hidden[...], far_hidden[...])
    gate = dot_nn(hidden, w_gate[...])
    up = dot_nn(hidden, w_up[...])
    gates[...] = gate.astype(BF16)
    ups[...] = up.astype(BF16)
    activated[...] = (gate * (1.0 / (1.0 + jnp.exp(-gate))) * up).astype(BF16)


def second_kernel(steps, *refs):
    near_cot, far_cot, gates, ups, activated, w_gate, w_up, w_down = refs[:8]
    grads, near_back, far_back, near_out, far_out = refs[-5:]
    units = w_down.shape[1]
    near = pl.program_id(0) < steps
    cot = jnp.where(near, near_cot[...], far_cot[...])
    grad = dot_nn(cot, w_down[...])
    gate, up = gates[...].astype(F32), ups[...].astype(F32)
    sigmoid = 1.0 / (1.0 + jnp.exp(-gate))
    to_gate = (grad * up * (sigmoid * (1.0 + gate * (1.0 - sigmoid)))).astype(BF16)
    to_up = (grad * (gate * sigmoid)).astype(BF16)
    grads[:, :units] = to_gate
    grads[:, units:] = to_up
    back = (dot_nt(to_gate, w_gate[...]) + dot_nt(to_up, w_up[...])).astype(BF16)
    out = dot_nt(activated[...], w_down[...]).astype(BF16)

    @pl.when(near)
    def _():
        near_back[...] = back
        near_out[...] = out

    @pl.when(jnp.logical_not(near))
    def _():
        far_back[...] = back
        far_out[...] = out


def feed_forward(second, part, parts, tokens, whole, weights, held):
    rows, width = tokens[0].shape
    units = weights[0].shape[1]
    tile = min(rows, 256)
    steps = rows // tile
    near = pl.BlockSpec((tile, width), lambda i: (jnp.minimum(i, steps - 1), 0))
    far = pl.BlockSpec((tile, width), lambda i: (jnp.maximum(i - steps, 0), 0))
    weight = pl.BlockSpec((width, units), lambda i: (0, 0), pipeline_mode=pl.Buffered(1))

    def of_whole(columns):
        return pl.BlockSpec((tile, columns), lambda i: (part * 2 * steps + i, 0))

    kept = (2 * units,) if second else (units,) * 3
    first_held = 2 + len(whole) + len(weights)
    products = 8 if second else 4
    return pl.pallas_call(
        functools.partial(second_kernel if second else first_kernel, steps),
        grid=(2 * steps,),
        in_specs=[near, far]
        + [of_whole(units)] * len(whole)
        + [weight] * len(weights)
        + [pl.BlockSpec(memory_space=pl.ANY)] * len(held),
        out_specs=[of_whole(n) for n in kept] + ([near, far] * 2 if second else []),
        out_shape=[jax.ShapeDtypeStruct((parts * 2 * rows, n), BF16) for n in kept]
        + [jax.ShapeDtypeStruct((rows, width), BF16)] * (4 if second else 0),
        input_output_aliases={first_held + i: i for i in range(len(held))},
        compiler_params=pltpu.CompilerParams(vmem_limit_bytes=58 * 2**20),
        cost_estimate=pl.CostEstimate(
            flops=2 * products * 2 * rows * width * units,
            bytes_accessed=2 * (2 * rows * width + len(weights) * width * units + 10 * rows * units),
            transcendentals=2 * rows * units,
        ),
        name="second_half" if second else "first_half",
    )(*tokens, *whole, *weights, *held)


def gradient_kernel(*refs, count, extra):
    side, tokens, right, result = refs[0], refs[1 : 1 + count], refs[1 + count], refs[-1]
    del side
    rows = tokens[0].shape[0]
    total = refs[2 + count][...].astype(F32) if extra else None
    for i in range(count):
        term = lax.dot_general(
            tokens[i][...], right[i * rows : (i + 1) * rows, :], (((0,), (0,)), ((), ())), preferred_element_type=F32
        )
        total = term if total is None else total + term
    result[...] = total.astype(BF16)


def gradient_half(side, tokens, right, units, column=0, extra=()):
    rows, width = tokens[0].shape
    count, half = len(tokens), width // 2
    tile = 256 if units % 256 == 0 else 128
    steps = units // tile
    out = pl.BlockSpec((half, tile), lambda j, side: (0, j))
    return pl.pallas_call(
        functools.partial(gradient_kernel, count=count, extra=len(extra)),
        grid_spec=pltpu.PrefetchScalarGridSpec(
            num_scalar_prefetch=1,
            grid=(steps,),
            in_specs=[
                pl.BlockSpec((rows, half), lambda j, side: (0, side[0]), pipeline_mode=pl.Buffered(1))
            ]
            * count
            + [pl.BlockSpec((count * rows, tile), lambda j, side: (0, column * steps + j))]
            + [out] * len(extra),
            out_specs=out,
        ),
        out_shape=jax.ShapeDtypeStruct((half, units), BF16),
        compiler_params=pltpu.CompilerParams(vmem_limit_bytes=40 * 2**20),
        cost_estimate=pl.CostEstimate(
            flops=2 * count * rows * half * units,
            bytes_accessed=2 * (count * rows * (half + units) + half * units),
            transcendentals=0,
        ),
        name="gradient_half",
    )(side.reshape(1).astype(jnp.int32), *tokens, right, *extra)


def split_kernel(core, left, right, kept, leaving):
    total = lax.dot_general(left[...], right[...], (((0,), (0,)), ((), ())), preferred_element_type=F32)
    groups, _, rows, _ = (kept.shape[0], 2, *kept.shape[1:])
    total = total.astype(BF16).reshape(groups, 2, rows, -1)
    first = core[0] == 0
    kept[...] = jnp.where(first, total[:, 0], total[:, 1])
    leaving[...] = jnp.where(first, total[:, 1], total[:, 0])


def split_gradient(core, left, right, groups):
    count, width = left.shape
    columns = right.shape[1]
    tile = 256
    rows = width // (2 * groups)
    out = pl.BlockSpec((groups, rows, tile), lambda j, core: (0, 0, j))
    return pl.pallas_call(
        split_kernel,
        grid_spec=pltpu.PrefetchScalarGridSpec(
            num_scalar_prefetch=1,
            grid=(columns // tile,),
            in_specs=[
                pl.BlockSpec((count, width), lambda j, core: (0, 0), pipeline_mode=pl.Buffered(1)),
                pl.BlockSpec((count, tile), lambda j, core: (0, j)),
            ],
            out_specs=[out, out],
        ),
        out_shape=[jax.ShapeDtypeStruct((groups, rows, columns), BF16)] * 2,
        compiler_params=pltpu.CompilerParams(vmem_limit_bytes=40 * 2**20),
        cost_estimate=pl.CostEstimate(
            flops=2 * count * width * columns,
            bytes_accessed=2 * (count * (width + columns) + width * columns),
            transcendentals=0,
        ),
        name="split_gradient",
    )(core.reshape(1).astype(jnp.int32), left, right)


def per_device(
    tokens,
    lengths,
    permutation,
    cotangent,
    norm1_gain,
    mixer_in,
    mixer_gate,
    conv_kernel,
    mixer_out,
    norm2_gain,
    ffn_gate,
    ffn_up,
    ffn_down,
):
    micro, length, width = tokens.shape
    count_b, count_z = lax.axis_size("b"), lax.axis_size("z")
    ia, ib, ic, iz = (lax.axis_index(n) for n in EVERY)
    place = ((ia * count_b + ib) * 2 + ic) * count_z + iz
    per_block = BLOCK // length
    blocks = permutation.shape[1]
    local = conv_kernel.shape[1]
    rows = micro * length

    dealt = lax.dynamic_slice_in_dim(permutation, place // per_block, 1, axis=1)[:, 0]
    own = dealt * per_block + place % per_block
    spots = jnp.arange(blocks, dtype=jnp.int32)

    def holder(piece):
        at = jnp.sum(jnp.where(permutation == (piece // per_block)[:, None], spots[None, :], 0), axis=1)
        return at * per_block + piece % per_block

    before = holder(jnp.maximum(own - 1, 0))
    last = blocks * per_block - 1
    behind = holder(jnp.minimum(own + 1, last))
    order = jnp.arange(lengths.shape[1], dtype=jnp.int32)
    offsets = jnp.sum(jnp.where(order[None, None, :] < order[None, :, None], lengths[:, None, :], 0), axis=2)
    position = own[:, None] * length + jnp.arange(length, dtype=jnp.int32)[None, :]
    is_start = jnp.any(position[:, :, None] == offsets[:, None, :], axis=2)
    was_start = jnp.any(position[:, :, None] - 1 == offsets[:, None, :], axis=2)
    keep_one = jnp.where(is_start, 0.0, 1.0).astype(F32)[:, :, None]
    keep_two = jnp.where(is_start | was_start, 0.0, 1.0).astype(F32)[:, :, None]

    units = -(-ffn_gate.shape[1] // 128) * 128
    spare = ((0, 0), (0, units - ffn_gate.shape[1]))

    def rows_of(pieces):
        return lax.all_gather(jnp.concatenate(pieces, axis=1), ("a", "b", "c"), axis=0, tiled=True)

    def told_at_once(value):
        return lax.all_gather(lax.all_gather(value, "z", axis=0), ("a", "b", "c"), axis=0)

    def in_plane(value):
        value = value.reshape(2, count_b, *value.shape[1:])
        mine = lax.dynamic_index_in_dim(value, ic, 0, keepdims=False)
        far = shift_by(lax.dynamic_index_in_dim(value, 1 - ic, 0, keepdims=False), "c", 1)
        value = in_order([mine, far], "c", 1)
        pieces = [lax.dynamic_index_in_dim(value, ib, 0, keepdims=False)]
        for s in range(1, count_b):
            leaving = lax.dynamic_index_in_dim(value, (ib + s) % count_b, 0, keepdims=False)
            pieces.append(shift_by(leaving, "b", s))
        return pieces

    def plane_rows(pieces):
        value = in_order(pieces, "b", 0)
        return value.reshape(-1, *value.shape[2:])

    bits = exchange_order()
    tap_count = conv_kernel.size
    told_rows = jnp.concatenate(
        [
            tokens[:, length - 2 :, :].reshape(micro * 2, width).astype(F32),
            jnp.pad(conv_kernel.reshape(1, tap_count), ((0, 0), (0, width - tap_count))),
        ]
    )[None]
    pad_g, pad_u, pad_d = (jnp.pad(w, spare) for w in (ffn_gate, ffn_up, ffn_down))
    z_in = pieces_of(mixer_in, "z")
    told_rows = told(told_rows, bits[:-3])
    far_cotangent = pieces_of(cotangent.reshape(rows, width), "b")
    before_at = [entry_of(before[m] ^ place) for m in range(micro)]
    behind_at = [(behind[m] // count_z, behind[m] % count_z) for m in range(micro)]
    z_in, told_rows, far_cotangent, mixer_gate, mixer_out, pad_g, before_at, behind_at = phase(
        z_in, told_rows, far_cotangent, mixer_gate, mixer_out, pad_g, before_at, behind_at
    )
    w_in = rows_of(z_in)
    z_gate = pieces_of(mixer_gate, "z")
    near_g = near_pieces(pad_g, "z")
    z_gate, near_g, told_rows, mixer_out, pad_u, pad_d = phase(z_gate, near_g, told_rows, mixer_out, pad_u, pad_d)
    w_gate = rows_of(z_gate)
    z_out = pieces_of(mixer_out, "z")
    z_g = far_pieces(pad_g, near_g, "z")
    told_rows = told(told_rows, bits[-3:-2])
    z_out, z_g, told_rows, pad_u, pad_d, w_in = phase(z_out, z_g, told_rows, pad_u, pad_d, w_in)
    w_out = rows_of(z_out)
    plane_g = in_plane(in_order(z_g, "z", 0))
    z_u = pieces_of(pad_u, "z")
    told_rows = told(told_rows, bits[-2:])
    plane_g, z_u, told_rows, pad_d, w_gate = phase(plane_g, z_u, told_rows, pad_d, w_gate)
    y_g = pieces_of(plane_rows(plane_g), "a")
    plane_u = in_plane(in_order(z_u, "z", 0))
    z_d = pieces_of(pad_d, "z")
    kernel = jnp.concatenate(
        [
            lax.dynamic_slice(
                told_rows, (entry_of(place ^ (place - iz + (iz - s) % count_z)), micro * 2, 0), (1, 1, tap_count)
            ).reshape(3, local)
            for s in range(count_z)
        ],
        axis=1,
    )
    y_g, plane_u, z_d, w_out = phase(y_g, plane_u, z_d, w_out)
    y_u = pieces_of(plane_rows(plane_u), "a")
    plane_d = in_plane(in_order(z_d, "z", 0))
    ffn_g = in_order(y_g, "a", 0).reshape(-1, units)

    tail_in = jnp.concatenate(
        [
            lax.dynamic_slice(told_rows, (before_at[m], 2 * m, 0), (1, 2, width))[0]
            for m in range(micro)
        ]
    )
    local_in = tokens.reshape(rows, width).astype(F32)
    local_cot = cotangent.reshape(rows, width).astype(F32)
    scale_one = lax.rsqrt(jnp.mean(local_in * local_in, axis=1, keepdims=True) + EPSILON)
    normed_one = local_in * scale_one
    hidden_one = (normed_one * norm1_gain).astype(BF16)
    tail_scale = lax.rsqrt(jnp.mean(tail_in * tail_in, axis=1, keepdims=True) + EPSILON)
    tail_hidden = (tail_in * tail_scale * norm1_gain).astype(BF16)
    channels = kernel.shape[1]
    signal = dot_nn(hidden_one, w_in).reshape(micro, length, channels)
    tail_signal = dot_nn(tail_hidden, w_in).reshape(micro, 2, channels)
    gating = dot_nn(hidden_one, w_gate).reshape(micro, length, channels)
    extended = jnp.concatenate([tail_signal, signal], axis=1)
    shift_one = keep_one * extended[:, 1 : length + 1, :]
    shift_two = keep_two * extended[:, 0:length, :]
    mixed = kernel[0] * signal + kernel[1] * shift_one + kernel[2] * shift_two
    product = (mixed * gating).astype(BF16).reshape(rows, channels)
    residual = local_in + dot_nt(product, w_out)

    scale_two = lax.rsqrt(jnp.mean(residual * residual, axis=1, keepdims=True) + EPSILON)
    normed_two = residual * scale_two
    hidden_own = (normed_two * norm2_gain).astype(BF16)


    def with_core(pieces):
        return [v for piece in pieces for v in (piece, shift_by(piece, "c", 1))]

    plane_d, y_u, ffn_g, hidden_own = phase(plane_d, y_u, ffn_g, hidden_own)
    y_d = pieces_of(plane_rows(plane_d), "a")
    ffn_u = in_order(y_u, "a", 0).reshape(-1, units)
    far_hidden = pieces_of(hidden_own, "b")[1:]
    hidden_parts = with_core([hidden_own])
    kept = feed_forward(False, 0, count_b, hidden_parts, (), (ffn_g, ffn_u), ())
    y_d, far_hidden, kept = phase(y_d, far_hidden, kept)
    hidden_parts = hidden_parts + with_core(far_hidden)
    for s in range(1, count_b):
        kept = feed_forward(False, s, count_b, hidden_parts[2 * s : 2 * s + 2], (), (ffn_g, ffn_u), kept)
    gates, ups, activated = kept
    ffn_d = in_order(y_d, "a", 0).reshape(-1, units)
    cot_parts = with_core(far_cotangent)
    other = 1 - ia
    leaving_down = gradient_half(other, cot_parts, activated, units)
    leaving_down, cot_parts, hidden_parts = phase(leaving_down, cot_parts, hidden_parts)
    come_down = shift_by(leaving_down, "a", 1)
    held, backs, outs = (), [None] * count_b, [None] * count_b
    for s in reversed(range(count_b)):
        pair = cot_parts[2 * s : 2 * s + 2]
        *held, near_back, far_back, near_out, far_out = feed_forward(
            True, s, count_b, pair, (gates, ups, activated), (ffn_g, ffn_u, ffn_d), held
        )
        backs[s] = (near_back, shift_by(far_back, "c", 1))
        outs[s] = (near_out, shift_by(far_out, "c", 1))
    grads = held[0]

    def to_owners(sums):
        return [(near.astype(F32) + far.astype(F32)).astype(BF16) for near, far in sums]

    def passed(values):
        return [shift_by(v, "b", -1 - i) for i, v in enumerate(values)]

    def over_z(stay, come):
        return lax.psum_scatter(joined([stay, come]).astype(BF16), "z", scatter_dimension=0, tiled=True)

    leaving_gate = gradient_half(other, hidden_parts, grads, units)
    own_back, own_out = backs[0], outs[0]
    leaving_gate, come_down, far_backs, far_outs, hidden_parts, cot_parts = phase(
        leaving_gate, come_down, backs[1:], outs[1:], hidden_parts, cot_parts
    )
    come_gate, came_back = shift_by(leaving_gate, "a", 1), passed(to_owners(far_backs))
    leaving_up = gradient_half(other, hidden_parts, grads, units, 1)
    stay_down = gradient_half(ia, cot_parts, activated, units)
    stay_gate = gradient_half(ia, hidden_parts, grads, units)
    stay_up = gradient_half(ia, hidden_parts, grads, units, 1)
    leaving_out = to_owners(far_outs)
    scattered_down = over_z(stay_down, come_down)
    come_gate, came_back, leaving_up, stay_gate, stay_up, own_back, own_out, leaving_out = phase(
        come_gate, came_back, leaving_up, stay_gate, stay_up, own_back, own_out, leaving_out
    )
    come_up, came_out = shift_by(leaving_up, "a", 1), passed(leaving_out)
    scattered_gate = over_z(stay_gate, come_gate)
    grad_hidden_two = joined([*own_back, *came_back])

    grad_gain_two = jnp.sum(grad_hidden_two * normed_two, axis=0)
    grad_norm_two = grad_hidden_two * norm2_gain
    inner_two = jnp.mean(grad_norm_two * normed_two, axis=1, keepdims=True)
    grad_residual = local_cot + scale_two * (grad_norm_two - normed_two * inner_two)
    grad_branch = grad_residual.astype(BF16)
    grad_product = dot_nn(grad_branch, w_out).reshape(micro, length, channels)
    def over_c(split):
        kept, leaving = split
        shape = (2, count_b, *kept.shape[1:])
        return [kept.reshape(shape), shift_by(leaving, "c", 1).reshape(shape)]

    def split(left, right):
        return split_gradient(ic, left, right, 2 * count_b)

    out_split = split(grad_branch, product)
    grad_mixed = grad_product * gating
    grad_gating = (grad_product * mixed).astype(BF16).reshape(rows, channels)
    grad_kernel = jnp.stack(
        [
            jnp.sum(grad_mixed * signal, axis=(0, 1)),
            jnp.sum(grad_mixed * shift_one, axis=(0, 1)),
            jnp.sum(grad_mixed * shift_two, axis=(0, 1)),
        ]
    )
    into_one = kernel[1] * (keep_one * grad_mixed)
    into_two = kernel[2] * (keep_two * grad_mixed)
    leaving = jnp.stack([into_two[:, 0], into_one[:, 0] + into_two[:, 1]], axis=1)
    blocked = leaving.reshape(micro, 2, count_z, local)

    def turned(value, dim):
        picks = [
            lax.dynamic_index_in_dim(value, (iz - j) % count_z, dim, keepdims=False) for j in range(count_z)
        ]
        return jnp.concatenate(picks, axis=-1)

    blocked = turned(blocked, 2).reshape(micro * 2, channels).astype(BF16)
    gate_split = split(hidden_one, grad_gating)
    from_gating = dot_nt(grad_gating, w_gate)
    blocked, come_up, came_out, out_split, gate_split, grad_mixed, from_gating, scattered_down = phase(
        blocked, come_up, came_out, out_split, gate_split, grad_mixed, from_gating, scattered_down
    )
    everyone = told_at_once(blocked)
    out_c, gate_c = over_c(out_split), over_c(gate_split)
    everyone, out_c, gate_c, grad_mixed, scattered_gate, scattered_down, come_up = phase(
        everyone, out_c, gate_c, grad_mixed, scattered_gate, scattered_down, come_up
    )
    scattered_up = over_z(stay_up, come_up)
    out_b = parted(out_c, "b", 1)
    gate_a = parted(gate_c, "a", 0)
    down_home = home(scattered_down)
    into_one = kernel[1] * (keep_one * grad_mixed)
    into_two = kernel[2] * (keep_two * grad_mixed)
    arrived = jnp.stack(
        [
            lax.dynamic_slice(
                everyone, (*behind_at[m], 2 * m, 0), (1, 1, 2, channels)
            )[0, 0]
            for m in range(micro)
        ]
    )
    arrived = turned(arrived.reshape(micro, 2, count_z, local), 2).astype(F32)
    arrived = jnp.where((own == last)[:, None, None], 0.0, arrived)
    from_one = jnp.concatenate([into_one[:, 1:], arrived[:, 1:]], axis=1)
    from_two = jnp.concatenate([into_two[:, 2:], arrived[:, :1], jnp.zeros_like(arrived[:, :1])], axis=1)
    grad_signal = (kernel[0] * grad_mixed + from_one + from_two).astype(BF16).reshape(rows, channels)
    in_split = split(hidden_one, grad_signal)
    grad_hidden_one = dot_nt(grad_signal, w_in) + from_gating
    grad_gain_one = jnp.sum(grad_hidden_one * normed_one, axis=0)
    grad_norm_one = grad_hidden_one * norm1_gain
    inner_one = jnp.mean(grad_norm_one * normed_one, axis=1, keepdims=True)
    input_grad = grad_residual + scale_one * (grad_norm_one - normed_one * inner_one)
    out_b, gate_a, in_split, input_grad, down_home, scattered_gate, grad_gain_one, own_out = phase(
        out_b, gate_a, in_split, input_grad, down_home, scattered_gate, grad_gain_one, own_out
    )
    in_c = over_c(in_split)
    middle = channels // 128 * 5 // 7 * 128
    in_a = parted([t[..., :middle] for t in in_c], "a", 0)
    in_b = parted([t[..., middle:] for t in in_c], "b", 1)
    gate_b = parted(settled(gate_a, "a", 0), "b", 0)
    out_a = parted(settled(out_b, "b", 1), "a", 0)
    gate_home, up_home = home(scattered_gate), home(scattered_up)
    by_place = (2, count_b, 2, count_z, -1)
    both_gains = jnp.stack([g.reshape(by_place) for g in (grad_gain_one, grad_gain_two)], axis=3)
    kernel_parts = turned(grad_kernel.reshape(3, count_z, local), 1).reshape(3, count_z, 2, count_b, 2, -1)
    small = jnp.concatenate([both_gains, kernel_parts.transpose(2, 3, 4, 0, 1, 5)], axis=3)
    small = parted([small], "c", 2, F32)
    in_a, in_b, gate_b, out_a, gate_home, up_home, down_home, own_out, small = phase(
        in_a, in_b, gate_b, out_a, gate_home, up_home, down_home, own_out, small
    )
    small = parted(settled(small, "c", 2), "a", 0, F32)
    small = parted(settled(small, "a", 0), "b", 0, F32)
    in_a, in_b = parted(settled(in_a, "a", 0), "b", 0), parted(settled(in_b, "b", 1), "a", 0)
    two_z = columns_home([jnp.concatenate([joined(settled(out_a, "a", 0)), joined(settled(gate_b, "b", 0))], axis=0)])
    in_a, in_b, two_z, small, own_out = phase(in_a, in_b, two_z, small, own_out)
    output = (joined([*own_out, *came_out]) + residual).astype(BF16)
    small = joined(settled(small, "b", 0))
    share = small.shape[2]
    small = turned(jnp.pad(small, ((0, 3), (0, 0), (0, local - share))), 1)
    in_rows = jnp.concatenate([joined(settled(in_a, "b", 0)), joined(settled(in_b, "a", 0))], axis=1)
    in_z = columns_home([jnp.concatenate([in_rows, small], axis=0)])
    grad_out, grad_gate_w = jnp.split(joined(two_z), 2)
    in_z = joined(in_z)
    grad_in_w, small = in_z[: in_rows.shape[0]], in_z[in_rows.shape[0] :, :share]
    hidden_units = ffn_gate.shape[1]
    grad_ffg, grad_ffu, grad_down = (g[:, :hidden_units].astype(F32) for g in (gate_home, up_home, down_home))

    return (
        output.reshape(micro, length, width),
        input_grad.reshape(micro, length, width),
        small[0],
        grad_in_w,
        grad_gate_w,
        small[2:5],
        grad_out,
        small[1],
        grad_ffg,
        grad_ffu,
        grad_down,
    )


def solution(mesh):
    row, col = mesh.shape["row"], mesh.shape["col"]
    fine = Mesh(mesh.devices.reshape(2, row // 4, 2, col), EVERY)
    by_rows = ("a", "b", "c")
    matrix = P(by_rows, "z")
    token = P(None, EVERY, None)
    return jax.shard_map(
        per_device,
        mesh=fine,
        in_specs=(
            token,
            P(),
            P(),
            token,
            P(),
            matrix,
            matrix,
            P(None, "z"),
            matrix,
            P(),
            matrix,
            matrix,
            matrix,
        ),
        out_specs=(
            token,
            token,
            P(EVERY),
            matrix,
            matrix,
            P(None, ("z", *by_rows)),
            matrix,
            P(EVERY),
            matrix,
            matrix,
            matrix,
        ),
        check_vma=False,
    )
```

```python
import functools

import jax
import jax.numpy as jnp
from jax import lax
from jax.experimental import pallas as pl
from jax.experimental.pallas import tpu as pltpu
from jax.sharding import Mesh
from jax.sharding import PartitionSpec as P

BLOCK = 128
EPSILON = 1e-05
F32 = jnp.float32
BF16 = jnp.bfloat16
EVERY = ("a", "b", "c", "z")


def dot_nn(left, right):
    return lax.dot_general(left, right, (((1,), (0,)), ((), ())), preferred_element_type=F32)


def dot_nt(left, right):
    return lax.dot_general(left, right, (((1,), (1,)), ((), ())), preferred_element_type=F32)


def dot_tn(left, right):
    return lax.dot_general(left, right, (((0,), (0,)), ((), ())), preferred_element_type=F32)


def shift_by(value, axis, amount):
    size = lax.axis_size(axis)
    return lax.ppermute(value, axis, [(i, (i + amount) % size) for i in range(size)])


def pieces_of(value, axis):
    return [value] + [shift_by(value, axis, s) for s in range(1, lax.axis_size(axis))]


def near_pieces(value, axis):
    return shift_by(value, axis, 1), shift_by(value, axis, -1)


def far_pieces(value, near, axis):
    size = lax.axis_size(axis)
    pieces = [value] + [None] * (size - 1)
    pieces[1], pieces[size - 1] = near
    for s in range(2, size // 2 + 1):
        pieces[s] = shift_by(pieces[s - 1], axis, 1)
    for s in range(2, (size - 1) // 2 + 1):
        pieces[size - s] = shift_by(pieces[size - s + 1], axis, -1)
    return pieces


def phase(*values):
    return lax.optimization_barrier(values)


def after(value, *earlier):
    return lax.optimization_barrier((value, earlier))[0]


def in_order(pieces, axis, dim):
    size, index = len(pieces), lax.axis_index(axis)
    if size == 2:
        first = index == 0
        return jnp.stack(
            [jnp.where(first, pieces[0], pieces[1]), jnp.where(first, pieces[1], pieces[0])], axis=dim
        )
    return jnp.stack(
        [lax.select_n((index - j) % size, *pieces) for j in range(size)], axis=dim
    )


def slices_of(terms, i, dim):
    return [lax.dynamic_index_in_dim(t, i, dim, keepdims=False) for t in terms]


def parted(terms, axis, dim, kind=BF16):
    size, index = lax.axis_size(axis), lax.axis_index(axis)
    return terms, [
        shift_by(joined(slices_of(terms, (index - s) % size, dim)).astype(kind), axis, -s) for s in range(1, size)
    ]


def settled(parts, axis, dim):
    terms, arrived = parts
    return slices_of(terms, lax.axis_index(axis), dim) + arrived


def joined(terms):
    total = terms[0].astype(F32)
    for value in terms[1:]:
        total = total + value.astype(F32)
    return total


def columns_home(terms):
    count = lax.axis_size("z")
    local = terms[0].shape[1] // count

    def columns(s):
        return joined([t[:, s * local : (s + 1) * local] for t in terms])

    return [columns(0)] + [shift_by(columns(s).astype(BF16), "z", -s) for s in range(1, count)]


def home(block):
    count, size = lax.axis_size("z"), lax.axis_size("b")
    moves = []
    for t in range(count):
        for z in range(count):
            team = (z % size) * 2 + z // size
            moves.append((team * count + t, t * count + z))
    return lax.ppermute(block, ("b", "c", "z"), moves)


def partner(value, bit):
    count = lax.axis_size(EVERY)
    return lax.ppermute(value, EVERY, [(i, i ^ bit) for i in range(count)])


def exchange_order():
    bits = [1 << i for i in range(lax.axis_size(EVERY).bit_length() - 1)]
    core = lax.axis_size("z")
    return [b for b in bits if b < core] + [b for b in bits[::-1] if b > core] + [core]


def entry_of(difference):
    return sum(((difference & bit) // bit) << i for i, bit in enumerate(exchange_order()))


def told(value, bits):
    for bit in bits:
        value = jnp.concatenate([value, partner(value, bit)], axis=0)
    return value


def first_kernel(steps, *refs):
    near_hidden, far_hidden, w_gate, w_up = refs[:4]
    gates, ups, activated = refs[-3:]
    near = pl.program_id(0) < steps
    hidden = jnp.where(near, near_hidden[...], far_hidden[...])
    gate = dot_nn(hidden, w_gate[...])
    up = dot_nn(hidden, w_up[...])
    gates[...] = gate.astype(BF16)
    ups[...] = up.astype(BF16)
    activated[...] = (gate * (1.0 / (1.0 + jnp.exp(-gate))) * up).astype(BF16)


def second_kernel(steps, *refs):
    near_cot, far_cot, gates, ups, activated, w_gate, w_up, w_down = refs[:8]
    grads, near_back, far_back, near_out, far_out = refs[-5:]
    units = w_down.shape[1]
    near = pl.program_id(0) < steps
    cot = jnp.where(near, near_cot[...], far_cot[...])
    grad = dot_nn(cot, w_down[...])
    gate, up = gates[...].astype(F32), ups[...].astype(F32)
    sigmoid = 1.0 / (1.0 + jnp.exp(-gate))
    to_gate = (grad * up * (sigmoid * (1.0 + gate * (1.0 - sigmoid)))).astype(BF16)
    to_up = (grad * (gate * sigmoid)).astype(BF16)
    grads[:, :units] = to_gate
    grads[:, units:] = to_up
    back = (dot_nt(to_gate, w_gate[...]) + dot_nt(to_up, w_up[...])).astype(BF16)
    out = dot_nt(activated[...], w_down[...]).astype(BF16)

    @pl.when(near)
    def _():
        near_back[...] = back
        near_out[...] = out

    @pl.when(jnp.logical_not(near))
    def _():
        far_back[...] = back
        far_out[...] = out


def feed_forward(second, part, parts, tokens, whole, weights, held):
    rows, width = tokens[0].shape
    units = weights[0].shape[1]
    tile = min(rows, 256)
    steps = rows // tile
    near = pl.BlockSpec((tile, width), lambda i: (jnp.minimum(i, steps - 1), 0))
    far = pl.BlockSpec((tile, width), lambda i: (jnp.maximum(i - steps, 0), 0))
    weight = pl.BlockSpec((width, units), lambda i: (0, 0), pipeline_mode=pl.Buffered(1))

    def of_whole(columns):
        return pl.BlockSpec((tile, columns), lambda i: (part * 2 * steps + i, 0))

    kept = (2 * units,) if second else (units,) * 3
    first_held = 2 + len(whole) + len(weights)
    products = 8 if second else 4
    return pl.pallas_call(
        functools.partial(second_kernel if second else first_kernel, steps),
        grid=(2 * steps,),
        in_specs=[near, far]
        + [of_whole(units)] * len(whole)
        + [weight] * len(weights)
        + [pl.BlockSpec(memory_space=pl.ANY)] * len(held),
        out_specs=[of_whole(n) for n in kept] + ([near, far] * 2 if second else []),
        out_shape=[jax.ShapeDtypeStruct((parts * 2 * rows, n), BF16) for n in kept]
        + [jax.ShapeDtypeStruct((rows, width), BF16)] * (4 if second else 0),
        input_output_aliases={first_held + i: i for i in range(len(held))},
        compiler_params=pltpu.CompilerParams(vmem_limit_bytes=58 * 2**20),
        cost_estimate=pl.CostEstimate(
            flops=2 * products * 2 * rows * width * units,
            bytes_accessed=2 * (2 * rows * width + len(weights) * width * units + 10 * rows * units),
            transcendentals=2 * rows * units,
        ),
        name="second_half" if second else "first_half",
    )(*tokens, *whole, *weights, *held)


def gradient_kernel(*refs, count, extra):
    side, tokens, right, result = refs[0], refs[1 : 1 + count], refs[1 + count], refs[-1]
    del side
    rows = tokens[0].shape[0]
    total = refs[2 + count][...].astype(F32) if extra else None
    for i in range(count):
        term = lax.dot_general(
            tokens[i][...], right[i * rows : (i + 1) * rows, :], (((0,), (0,)), ((), ())), preferred_element_type=F32
        )
        total = term if total is None else total + term
    result[...] = total.astype(BF16)


def gradient_half(side, tokens, right, units, column=0, extra=()):
    rows, width = tokens[0].shape
    count, half = len(tokens), width // 2
    tile = 256 if units % 256 == 0 else 128
    steps = units // tile
    out = pl.BlockSpec((half, tile), lambda j, side: (0, j))
    return pl.pallas_call(
        functools.partial(gradient_kernel, count=count, extra=len(extra)),
        grid_spec=pltpu.PrefetchScalarGridSpec(
            num_scalar_prefetch=1,
            grid=(steps,),
            in_specs=[
                pl.BlockSpec((rows, half), lambda j, side: (0, side[0]), pipeline_mode=pl.Buffered(1))
            ]
            * count
            + [pl.BlockSpec((count * rows, tile), lambda j, side: (0, column * steps + j))]
            + [out] * len(extra),
            out_specs=out,
        ),
        out_shape=jax.ShapeDtypeStruct((half, units), BF16),
        compiler_params=pltpu.CompilerParams(vmem_limit_bytes=40 * 2**20),
        cost_estimate=pl.CostEstimate(
            flops=2 * count * rows * half * units,
            bytes_accessed=2 * (count * rows * (half + units) + half * units),
            transcendentals=0,
        ),
        name="gradient_half",
    )(side.reshape(1).astype(jnp.int32), *tokens, right, *extra)


def split_kernel(core, left, right, kept, leaving):
    total = lax.dot_general(left[...], right[...], (((0,), (0,)), ((), ())), preferred_element_type=F32)
    groups, _, rows, _ = (kept.shape[0], 2, *kept.shape[1:])
    total = total.astype(BF16).reshape(groups, 2, rows, -1)
    first = core[0] == 0
    kept[...] = jnp.where(first, total[:, 0], total[:, 1])
    leaving[...] = jnp.where(first, total[:, 1], total[:, 0])


def split_gradient(core, left, right, groups):
    count, width = left.shape
    columns = right.shape[1]
    tile = 256
    rows = width // (2 * groups)
    out = pl.BlockSpec((groups, rows, tile), lambda j, core: (0, 0, j))
    return pl.pallas_call(
        split_kernel,
        grid_spec=pltpu.PrefetchScalarGridSpec(
            num_scalar_prefetch=1,
            grid=(columns // tile,),
            in_specs=[
                pl.BlockSpec((count, width), lambda j, core: (0, 0), pipeline_mode=pl.Buffered(1)),
                pl.BlockSpec((count, tile), lambda j, core: (0, j)),
            ],
            out_specs=[out, out],
        ),
        out_shape=[jax.ShapeDtypeStruct((groups, rows, columns), BF16)] * 2,
        compiler_params=pltpu.CompilerParams(vmem_limit_bytes=40 * 2**20),
        cost_estimate=pl.CostEstimate(
            flops=2 * count * width * columns,
            bytes_accessed=2 * (count * (width + columns) + width * columns),
            transcendentals=0,
        ),
        name="split_gradient",
    )(core.reshape(1).astype(jnp.int32), left, right)


def per_device(
    tokens,
    lengths,
    permutation,
    cotangent,
    norm1_gain,
    mixer_in,
    mixer_gate,
    conv_kernel,
    mixer_out,
    norm2_gain,
    ffn_gate,
    ffn_up,
    ffn_down,
):
    micro, length, width = tokens.shape
    count_b, count_z = lax.axis_size("b"), lax.axis_size("z")
    ia, ib, ic, iz = (lax.axis_index(n) for n in EVERY)
    place = ((ia * count_b + ib) * 2 + ic) * count_z + iz
    per_block = BLOCK // length
    blocks = permutation.shape[1]
    local = conv_kernel.shape[1]
    rows = micro * length

    dealt = lax.dynamic_slice_in_dim(permutation, place // per_block, 1, axis=1)[:, 0]
    own = dealt * per_block + place % per_block
    spots = jnp.arange(blocks, dtype=jnp.int32)

    def holder(piece):
        at = jnp.sum(jnp.where(permutation == (piece // per_block)[:, None], spots[None, :], 0), axis=1)
        return at * per_block + piece % per_block

    before = holder(jnp.maximum(own - 1, 0))
    last = blocks * per_block - 1
    behind = holder(jnp.minimum(own + 1, last))
    order = jnp.arange(lengths.shape[1], dtype=jnp.int32)
    offsets = jnp.sum(jnp.where(order[None, None, :] < order[None, :, None], lengths[:, None, :], 0), axis=2)
    position = own[:, None] * length + jnp.arange(length, dtype=jnp.int32)[None, :]
    is_start = jnp.any(position[:, :, None] == offsets[:, None, :], axis=2)
    was_start = jnp.any(position[:, :, None] - 1 == offsets[:, None, :], axis=2)
    keep_one = jnp.where(is_start, 0.0, 1.0).astype(F32)[:, :, None]
    keep_two = jnp.where(is_start | was_start, 0.0, 1.0).astype(F32)[:, :, None]

    units = -(-ffn_gate.shape[1] // 128) * 128
    spare = ((0, 0), (0, units - ffn_gate.shape[1]))

    def rows_of(pieces):
        return lax.all_gather(jnp.concatenate(pieces, axis=1), ("a", "b", "c"), axis=0, tiled=True)

    def told_at_once(value):
        return lax.all_gather(lax.all_gather(value, "z", axis=0), ("a", "b", "c"), axis=0)

    def in_plane(value):
        value = value.reshape(2, count_b, *value.shape[1:])
        mine = lax.dynamic_index_in_dim(value, ic, 0, keepdims=False)
        far = shift_by(lax.dynamic_index_in_dim(value, 1 - ic, 0, keepdims=False), "c", 1)
        value = in_order([mine, far], "c", 1)
        pieces = [lax.dynamic_index_in_dim(value, ib, 0, keepdims=False)]
        for s in range(1, count_b):
            leaving = lax.dynamic_index_in_dim(value, (ib + s) % count_b, 0, keepdims=False)
            pieces.append(shift_by(leaving, "b", s))
        return pieces

    def plane_rows(pieces):
        value = in_order(pieces, "b", 0)
        return value.reshape(-1, *value.shape[2:])

    bits = exchange_order()
    told_rows = tokens[:, length - 2 :, :].reshape(1, micro * 2, width)
    pad_g, pad_u, pad_d = (jnp.pad(w, spare) for w in (ffn_gate, ffn_up, ffn_down))
    z_in = pieces_of(mixer_in, "z")
    z_bits = [b for b in bits if b < count_z]
    told_rows = told(told_rows, z_bits)
    taps = told(conv_kernel[None], z_bits)
    far_cotangent = pieces_of(cotangent.reshape(rows, width), "b")
    before_at = [entry_of(before[m] ^ place) for m in range(micro)]
    behind_at = [(behind[m] // count_z, behind[m] % count_z) for m in range(micro)]
    z_in, told_rows, taps, far_cotangent, mixer_gate, mixer_out, pad_g, before_at, behind_at = phase(
        z_in, told_rows, taps, far_cotangent, mixer_gate, mixer_out, pad_g, before_at, behind_at
    )
    w_in = rows_of(z_in)
    z_gate = pieces_of(mixer_gate, "z")
    near_g = near_pieces(pad_g, "z")
    z_gate, near_g, told_rows, mixer_out, pad_u, pad_d = phase(z_gate, near_g, told_rows, mixer_out, pad_u, pad_d)
    w_gate = rows_of(z_gate)
    z_out = pieces_of(mixer_out, "z")
    z_g = far_pieces(pad_g, near_g, "z")
    told_rows = told(told_rows, bits[len(z_bits) : -2])
    z_out, z_g, told_rows, pad_u, pad_d, w_in = phase(z_out, z_g, told_rows, pad_u, pad_d, w_in)
    w_out = rows_of(z_out)
    plane_g = in_plane(in_order(z_g, "z", 0))
    z_u = pieces_of(pad_u, "z")
    told_rows = told(told_rows, bits[-2:])
    plane_g, z_u, told_rows, pad_d, w_gate = phase(plane_g, z_u, told_rows, pad_d, w_gate)
    y_g = pieces_of(plane_rows(plane_g), "a")
    plane_u = in_plane(in_order(z_u, "z", 0))
    z_d = pieces_of(pad_d, "z")
    kernel = jnp.concatenate(
        [
            lax.dynamic_index_in_dim(taps, iz ^ ((iz - s) % count_z), 0, keepdims=False)
            for s in range(count_z)
        ],
        axis=1,
    )
    y_g, plane_u, z_d, w_out = phase(y_g, plane_u, z_d, w_out)
    y_u = pieces_of(plane_rows(plane_u), "a")
    plane_d = in_plane(in_order(z_d, "z", 0))
    ffn_g = in_order(y_g, "a", 0).reshape(-1, units)

    tail_in = jnp.concatenate(
        [
            lax.dynamic_slice(told_rows, (before_at[m], 2 * m, 0), (1, 2, width))[0]
            for m in range(micro)
        ]
    ).astype(F32)
    local_in = tokens.reshape(rows, width).astype(F32)
    local_cot = cotangent.reshape(rows, width).astype(F32)
    scale_one = lax.rsqrt(jnp.mean(local_in * local_in, axis=1, keepdims=True) + EPSILON)
    normed_one = local_in * scale_one
    hidden_one = (normed_one * norm1_gain).astype(BF16)
    tail_scale = lax.rsqrt(jnp.mean(tail_in * tail_in, axis=1, keepdims=True) + EPSILON)
    tail_hidden = (tail_in * tail_scale * norm1_gain).astype(BF16)
    channels = kernel.shape[1]
    signal = dot_nn(hidden_one, w_in).reshape(micro, length, channels)
    tail_signal = dot_nn(tail_hidden, w_in).reshape(micro, 2, channels)
    gating = dot_nn(hidden_one, w_gate).reshape(micro, length, channels)
    extended = jnp.concatenate([tail_signal, signal], axis=1)
    shift_one = keep_one * extended[:, 1 : length + 1, :]
    shift_two = keep_two * extended[:, 0:length, :]
    mixed = kernel[0] * signal + kernel[1] * shift_one + kernel[2] * shift_two
    product = (mixed * gating).astype(BF16).reshape(rows, channels)
    residual = local_in + dot_nt(product, w_out)

    scale_two = lax.rsqrt(jnp.mean(residual * residual, axis=1, keepdims=True) + EPSILON)
    normed_two = residual * scale_two
    hidden_own = (normed_two * norm2_gain).astype(BF16)


    def with_core(pieces):
        return [v for piece in pieces for v in (piece, shift_by(piece, "c", 1))]

    plane_d, y_u, ffn_g, hidden_own = phase(plane_d, y_u, ffn_g, hidden_own)
    y_d = pieces_of(plane_rows(plane_d), "a")
    ffn_u = in_order(y_u, "a", 0).reshape(-1, units)
    far_hidden = pieces_of(hidden_own, "b")[1:]
    hidden_parts = with_core([hidden_own])
    kept = feed_forward(False, 0, count_b, hidden_parts, (), (ffn_g, ffn_u), ())
    y_d, far_hidden, kept = phase(y_d, far_hidden, kept)
    hidden_parts = hidden_parts + with_core(far_hidden)
    for s in range(1, count_b):
        kept = feed_forward(False, s, count_b, hidden_parts[2 * s : 2 * s + 2], (), (ffn_g, ffn_u), kept)
    gates, ups, activated = kept
    ffn_d = in_order(y_d, "a", 0).reshape(-1, units)
    cot_parts = with_core(far_cotangent)
    other = 1 - ia
    leaving_down = gradient_half(other, cot_parts, activated, units)
    leaving_down, cot_parts, hidden_parts = phase(leaving_down, cot_parts, hidden_parts)
    come_down = shift_by(leaving_down, "a", 1)
    held, backs, outs = (), [None] * count_b, [None] * count_b
    for s in reversed(range(count_b)):
        pair = cot_parts[2 * s : 2 * s + 2]
        *held, near_back, far_back, near_out, far_out = feed_forward(
            True, s, count_b, pair, (gates, ups, activated), (ffn_g, ffn_u, ffn_d), held
        )
        backs[s] = (near_back, shift_by(far_back, "c", 1))
        outs[s] = (near_out, shift_by(far_out, "c", 1))
    grads = held[0]

    def to_owners(sums):
        return [(near.astype(F32) + far.astype(F32)).astype(BF16) for near, far in sums]

    def passed(values):
        return [shift_by(v, "b", -1 - i) for i, v in enumerate(values)]

    def over_z(stay, come):
        return lax.psum_scatter(joined([stay, come]).astype(BF16), "z", scatter_dimension=0, tiled=True)

    leaving_gate = gradient_half(other, hidden_parts, grads, units)
    own_back, own_out = backs[0], outs[0]
    leaving_gate, come_down, far_backs, far_outs, hidden_parts, cot_parts = phase(
        leaving_gate, come_down, backs[1:], outs[1:], hidden_parts, cot_parts
    )
    come_gate, came_back = shift_by(leaving_gate, "a", 1), passed(to_owners(far_backs))
    leaving_up = gradient_half(other, hidden_parts, grads, units, 1)
    stay_down = gradient_half(ia, cot_parts, activated, units)
    stay_gate = gradient_half(ia, hidden_parts, grads, units)
    stay_up = gradient_half(ia, hidden_parts, grads, units, 1)
    leaving_out = to_owners(far_outs)
    scattered_down = over_z(stay_down, come_down)
    come_gate, came_back, leaving_up, stay_gate, stay_up, own_back, own_out, leaving_out = phase(
        come_gate, came_back, leaving_up, stay_gate, stay_up, own_back, own_out, leaving_out
    )
    come_up, came_out = shift_by(leaving_up, "a", 1), passed(leaving_out)
    scattered_gate = over_z(stay_gate, come_gate)
    grad_hidden_two = joined([*own_back, *came_back])

    grad_gain_two = jnp.sum(grad_hidden_two * normed_two, axis=0)
    grad_norm_two = grad_hidden_two * norm2_gain
    inner_two = jnp.mean(grad_norm_two * normed_two, axis=1, keepdims=True)
    grad_residual = local_cot + scale_two * (grad_norm_two - normed_two * inner_two)
    grad_branch = grad_residual.astype(BF16)
    grad_product = dot_nn(grad_branch, w_out).reshape(micro, length, channels)
    def over_c(split):
        kept, leaving = split
        shape = (2, count_b, *kept.shape[1:])
        return [kept.reshape(shape), shift_by(leaving, "c", 1).reshape(shape)]

    def split(left, right):
        return split_gradient(ic, left, right, 2 * count_b)

    out_split = split(grad_branch, product)
    grad_mixed = grad_product * gating
    grad_gating = (grad_product * mixed).astype(BF16).reshape(rows, channels)
    grad_kernel = jnp.stack(
        [
            jnp.sum(grad_mixed * signal, axis=(0, 1)),
            jnp.sum(grad_mixed * shift_one, axis=(0, 1)),
            jnp.sum(grad_mixed * shift_two, axis=(0, 1)),
        ]
    )
    into_one = kernel[1] * (keep_one * grad_mixed)
    into_two = kernel[2] * (keep_two * grad_mixed)
    leaving = jnp.stack([into_two[:, 0], into_one[:, 0] + into_two[:, 1]], axis=1)
    blocked = leaving.reshape(micro, 2, count_z, local)

    def turned(value, dim):
        picks = [
            lax.dynamic_index_in_dim(value, (iz - j) % count_z, dim, keepdims=False) for j in range(count_z)
        ]
        return jnp.concatenate(picks, axis=-1)

    blocked = turned(blocked, 2).reshape(micro * 2, channels).astype(BF16)
    gate_split = split(hidden_one, grad_gating)
    from_gating = dot_nt(grad_gating, w_gate)
    blocked, come_up, came_out, out_split, gate_split, grad_mixed, from_gating, scattered_down = phase(
        blocked, come_up, came_out, out_split, gate_split, grad_mixed, from_gating, scattered_down
    )
    everyone = told_at_once(blocked)
    out_c, gate_c = over_c(out_split), over_c(gate_split)
    everyone, out_c, gate_c, grad_mixed, scattered_gate, scattered_down, come_up = phase(
        everyone, out_c, gate_c, grad_mixed, scattered_gate, scattered_down, come_up
    )
    scattered_up = over_z(stay_up, come_up)
    out_b = parted(out_c, "b", 1)
    gate_a = parted(gate_c, "a", 0)
    down_home = home(scattered_down)
    into_one = kernel[1] * (keep_one * grad_mixed)
    into_two = kernel[2] * (keep_two * grad_mixed)
    arrived = jnp.stack(
        [
            lax.dynamic_slice(
                everyone, (*behind_at[m], 2 * m, 0), (1, 1, 2, channels)
            )[0, 0]
            for m in range(micro)
        ]
    )
    arrived = turned(arrived.reshape(micro, 2, count_z, local), 2).astype(F32)
    arrived = jnp.where((own == last)[:, None, None], 0.0, arrived)
    from_one = jnp.concatenate([into_one[:, 1:], arrived[:, 1:]], axis=1)
    from_two = jnp.concatenate([into_two[:, 2:], arrived[:, :1], jnp.zeros_like(arrived[:, :1])], axis=1)
    grad_signal = (kernel[0] * grad_mixed + from_one + from_two).astype(BF16).reshape(rows, channels)
    in_split = split(hidden_one, grad_signal)
    grad_hidden_one = dot_nt(grad_signal, w_in) + from_gating
    grad_gain_one = jnp.sum(grad_hidden_one * normed_one, axis=0)
    grad_norm_one = grad_hidden_one * norm1_gain
    inner_one = jnp.mean(grad_norm_one * normed_one, axis=1, keepdims=True)
    input_grad = grad_residual + scale_one * (grad_norm_one - normed_one * inner_one)
    out_b, gate_a, in_split, input_grad, down_home, scattered_gate, grad_gain_one, own_out = phase(
        out_b, gate_a, in_split, input_grad, down_home, scattered_gate, grad_gain_one, own_out
    )
    in_c = over_c(in_split)
    middle = channels // 128 * 5 // 7 * 128
    in_a = parted([t[..., :middle] for t in in_c], "a", 0)
    in_b = parted([t[..., middle:] for t in in_c], "b", 1)
    gate_b = parted(settled(gate_a, "a", 0), "b", 0)
    out_a = parted(settled(out_b, "b", 1), "a", 0)
    gate_home, up_home = home(scattered_gate), home(scattered_up)
    by_place = (2, count_b, 2, count_z, -1)
    both_gains = jnp.stack([g.reshape(by_place) for g in (grad_gain_one, grad_gain_two)], axis=3)
    kernel_parts = turned(grad_kernel.reshape(3, count_z, local), 1).reshape(3, count_z, 2, count_b, 2, -1)
    small = jnp.concatenate([both_gains, kernel_parts.transpose(2, 3, 4, 0, 1, 5)], axis=3)
    small = parted([small], "c", 2, F32)
    in_a, in_b, gate_b, out_a, gate_home, up_home, down_home, own_out, small = phase(
        in_a, in_b, gate_b, out_a, gate_home, up_home, down_home, own_out, small
    )
    small = parted(settled(small, "c", 2), "a", 0, F32)
    small = parted(settled(small, "a", 0), "b", 0, F32)
    in_a, in_b = parted(settled(in_a, "a", 0), "b", 0), parted(settled(in_b, "b", 1), "a", 0)
    two_z = columns_home([jnp.concatenate([joined(settled(out_a, "a", 0)), joined(settled(gate_b, "b", 0))], axis=0)])
    in_a, in_b, two_z, small, own_out = phase(in_a, in_b, two_z, small, own_out)
    output = (joined([*own_out, *came_out]) + residual).astype(BF16)
    small = joined(settled(small, "b", 0))
    share = small.shape[2]
    small = turned(jnp.pad(small, ((0, 3), (0, 0), (0, local - share))), 1)
    in_rows = jnp.concatenate([joined(settled(in_a, "b", 0)), joined(settled(in_b, "a", 0))], axis=1)
    in_z = columns_home([jnp.concatenate([in_rows, small], axis=0)])
    grad_out, grad_gate_w = jnp.split(joined(two_z), 2)
    in_z = joined(in_z)
    grad_in_w, small = in_z[: in_rows.shape[0]], in_z[in_rows.shape[0] :, :share]
    hidden_units = ffn_gate.shape[1]
    grad_ffg, grad_ffu, grad_down = (g[:, :hidden_units].astype(F32) for g in (gate_home, up_home, down_home))

    return (
        output.reshape(micro, length, width),
        input_grad.reshape(micro, length, width),
        small[0],
        grad_in_w,
        grad_gate_w,
        small[2:5],
        grad_out,
        small[1],
        grad_ffg,
        grad_ffu,
        grad_down,
    )


def solution(mesh):
    row, col = mesh.shape["row"], mesh.shape["col"]
    fine = Mesh(mesh.devices.reshape(2, row // 4, 2, col), EVERY)
    by_rows = ("a", "b", "c")
    matrix = P(by_rows, "z")
    token = P(None, EVERY, None)
    return jax.shard_map(
        per_device,
        mesh=fine,
        in_specs=(
            token,
            P(),
            P(),
            token,
            P(),
            matrix,
            matrix,
            P(None, "z"),
            matrix,
            P(),
            matrix,
            matrix,
            matrix,
        ),
        out_specs=(
            token,
            token,
            P(EVERY),
            matrix,
            matrix,
            P(None, ("z", *by_rows)),
            matrix,
            P(EVERY),
            matrix,
            matrix,
            matrix,
        ),
        check_vma=False,
    )
```

```python
import functools

import jax
import jax.numpy as jnp
from jax import lax
from jax.experimental import pallas as pl
from jax.experimental.pallas import tpu as pltpu
from jax.sharding import Mesh
from jax.sharding import PartitionSpec as P

BLOCK = 128
EPSILON = 1e-05
F32 = jnp.float32
BF16 = jnp.bfloat16
EVERY = ("a", "b", "c", "z")


def dot_nn(left, right):
    return lax.dot_general(left, right, (((1,), (0,)), ((), ())), preferred_element_type=F32)


def dot_nt(left, right):
    return lax.dot_general(left, right, (((1,), (1,)), ((), ())), preferred_element_type=F32)


def dot_tn(left, right):
    return lax.dot_general(left, right, (((0,), (0,)), ((), ())), preferred_element_type=F32)


def shift_by(value, axis, amount):
    size = lax.axis_size(axis)
    return lax.ppermute(value, axis, [(i, (i + amount) % size) for i in range(size)])


def pieces_of(value, axis):
    return [value] + [shift_by(value, axis, s) for s in range(1, lax.axis_size(axis))]


def near_pieces(value, axis):
    return shift_by(value, axis, 1), shift_by(value, axis, -1)


def far_pieces(value, near, axis):
    size = lax.axis_size(axis)
    pieces = [value] + [None] * (size - 1)
    pieces[1], pieces[size - 1] = near
    for s in range(2, size // 2 + 1):
        pieces[s] = shift_by(pieces[s - 1], axis, 1)
    for s in range(2, (size - 1) // 2 + 1):
        pieces[size - s] = shift_by(pieces[size - s + 1], axis, -1)
    return pieces


def phase(*values):
    return lax.optimization_barrier(values)


def after(value, *earlier):
    return lax.optimization_barrier((value, earlier))[0]


def in_order(pieces, axis, dim):
    size, index = len(pieces), lax.axis_index(axis)
    if size == 2:
        first = index == 0
        return jnp.stack(
            [jnp.where(first, pieces[0], pieces[1]), jnp.where(first, pieces[1], pieces[0])], axis=dim
        )
    return jnp.stack(
        [lax.select_n((index - j) % size, *pieces) for j in range(size)], axis=dim
    )


def slices_of(terms, i, dim):
    return [lax.dynamic_index_in_dim(t, i, dim, keepdims=False) for t in terms]


def parted(terms, axis, dim, kind=BF16):
    size, index = lax.axis_size(axis), lax.axis_index(axis)
    return terms, [
        shift_by(joined(slices_of(terms, (index - s) % size, dim)).astype(kind), axis, -s) for s in range(1, size)
    ]


def settled(parts, axis, dim):
    terms, arrived = parts
    return slices_of(terms, lax.axis_index(axis), dim) + arrived


def joined(terms):
    total = terms[0].astype(F32)
    for value in terms[1:]:
        total = total + value.astype(F32)
    return total


def columns_home(terms):
    count = lax.axis_size("z")
    local = terms[0].shape[1] // count

    def columns(s):
        return joined([t[:, s * local : (s + 1) * local] for t in terms])

    return [columns(0)] + [shift_by(columns(s).astype(BF16), "z", -s) for s in range(1, count)]


def home(block):
    count, size = lax.axis_size("z"), lax.axis_size("b")
    moves = []
    for t in range(count):
        for z in range(count):
            team = (z % size) * 2 + z // size
            moves.append((team * count + t, t * count + z))
    return lax.ppermute(block, ("b", "c", "z"), moves)


def partner(value, bit):
    count = lax.axis_size(EVERY)
    return lax.ppermute(value, EVERY, [(i, i ^ bit) for i in range(count)])


def exchange_order():
    bits = [1 << i for i in range(lax.axis_size(EVERY).bit_length() - 1)]
    core = lax.axis_size("z")
    return [b for b in bits if b < core] + [b for b in bits[::-1] if b > core] + [core]


def entry_of(difference):
    return sum(((difference & bit) // bit) << i for i, bit in enumerate(exchange_order()))


def told(value, bits):
    for bit in bits:
        value = jnp.concatenate([value, partner(value, bit)], axis=0)
    return value


def first_kernel(steps, *refs):
    near_hidden, far_hidden, w_gate, w_up = refs[:4]
    gates, ups, activated = refs[-3:]
    near = pl.program_id(0) < steps
    hidden = jnp.where(near, near_hidden[...], far_hidden[...])
    gate = dot_nn(hidden, w_gate[...])
    up = dot_nn(hidden, w_up[...])
    gates[...] = gate.astype(BF16)
    ups[...] = up.astype(BF16)
    activated[...] = (gate * (1.0 / (1.0 + jnp.exp(-gate))) * up).astype(BF16)


def second_kernel(steps, *refs):
    near_cot, far_cot, gates, ups, activated, w_gate, w_up, w_down = refs[:8]
    grads, near_back, far_back, near_out, far_out = refs[-5:]
    units = w_down.shape[1]
    near = pl.program_id(0) < steps
    cot = jnp.where(near, near_cot[...], far_cot[...])
    grad = dot_nn(cot, w_down[...])
    gate, up = gates[...].astype(F32), ups[...].astype(F32)
    sigmoid = 1.0 / (1.0 + jnp.exp(-gate))
    to_gate = (grad * up * (sigmoid * (1.0 + gate * (1.0 - sigmoid)))).astype(BF16)
    to_up = (grad * (gate * sigmoid)).astype(BF16)
    grads[:, :units] = to_gate
    grads[:, units:] = to_up
    back = (dot_nt(to_gate, w_gate[...]) + dot_nt(to_up, w_up[...])).astype(BF16)
    out = dot_nt(activated[...], w_down[...]).astype(BF16)

    @pl.when(near)
    def _():
        near_back[...] = back
        near_out[...] = out

    @pl.when(jnp.logical_not(near))
    def _():
        far_back[...] = back
        far_out[...] = out


def feed_forward(second, part, parts, tokens, whole, weights, held):
    rows, width = tokens[0].shape
    units = weights[0].shape[1]
    tile = min(rows, 256)
    steps = rows // tile
    near = pl.BlockSpec((tile, width), lambda i: (jnp.minimum(i, steps - 1), 0))
    far = pl.BlockSpec((tile, width), lambda i: (jnp.maximum(i - steps, 0), 0))
    weight = pl.BlockSpec((width, units), lambda i: (0, 0), pipeline_mode=pl.Buffered(1))

    def of_whole(columns):
        return pl.BlockSpec((tile, columns), lambda i: (part * 2 * steps + i, 0))

    kept = (2 * units,) if second else (units,) * 3
    first_held = 2 + len(whole) + len(weights)
    products = 8 if second else 4
    return pl.pallas_call(
        functools.partial(second_kernel if second else first_kernel, steps),
        grid=(2 * steps,),
        in_specs=[near, far]
        + [of_whole(units)] * len(whole)
        + [weight] * len(weights)
        + [pl.BlockSpec(memory_space=pl.ANY)] * len(held),
        out_specs=[of_whole(n) for n in kept] + ([near, far] * 2 if second else []),
        out_shape=[jax.ShapeDtypeStruct((parts * 2 * rows, n), BF16) for n in kept]
        + [jax.ShapeDtypeStruct((rows, width), BF16)] * (4 if second else 0),
        input_output_aliases={first_held + i: i for i in range(len(held))},
        compiler_params=pltpu.CompilerParams(vmem_limit_bytes=58 * 2**20),
        cost_estimate=pl.CostEstimate(
            flops=2 * products * 2 * rows * width * units,
            bytes_accessed=2 * (2 * rows * width + len(weights) * width * units + 10 * rows * units),
            transcendentals=2 * rows * units,
        ),
        name="second_half" if second else "first_half",
    )(*tokens, *whole, *weights, *held)


def gradient_kernel(*refs, count, extra):
    side, tokens, right, result = refs[0], refs[1 : 1 + count], refs[1 + count], refs[-1]
    del side
    rows = tokens[0].shape[0]
    total = refs[2 + count][...].astype(F32) if extra else None
    for i in range(count):
        term = lax.dot_general(
            tokens[i][...], right[i * rows : (i + 1) * rows, :], (((0,), (0,)), ((), ())), preferred_element_type=F32
        )
        total = term if total is None else total + term
    result[...] = total.astype(BF16)


def gradient_half(side, tokens, right, units, column=0, extra=()):
    rows, width = tokens[0].shape
    count, half = len(tokens), width // 2
    tile = 256 if units % 256 == 0 else 128
    steps = units // tile
    out = pl.BlockSpec((half, tile), lambda j, side: (0, j))
    return pl.pallas_call(
        functools.partial(gradient_kernel, count=count, extra=len(extra)),
        grid_spec=pltpu.PrefetchScalarGridSpec(
            num_scalar_prefetch=1,
            grid=(steps,),
            in_specs=[
                pl.BlockSpec((rows, half), lambda j, side: (0, side[0]), pipeline_mode=pl.Buffered(1))
            ]
            * count
            + [pl.BlockSpec((count * rows, tile), lambda j, side: (0, column * steps + j))]
            + [out] * len(extra),
            out_specs=out,
        ),
        out_shape=jax.ShapeDtypeStruct((half, units), BF16),
        compiler_params=pltpu.CompilerParams(vmem_limit_bytes=40 * 2**20),
        cost_estimate=pl.CostEstimate(
            flops=2 * count * rows * half * units,
            bytes_accessed=2 * (count * rows * (half + units) + half * units),
            transcendentals=0,
        ),
        name="gradient_half",
    )(side.reshape(1).astype(jnp.int32), *tokens, right, *extra)


def split_kernel(core, left, right, kept, leaving):
    total = lax.dot_general(left[...], right[...], (((0,), (0,)), ((), ())), preferred_element_type=F32)
    groups, _, rows, _ = (kept.shape[0], 2, *kept.shape[1:])
    total = total.astype(BF16).reshape(groups, 2, rows, -1)
    first = core[0] == 0
    kept[...] = jnp.where(first, total[:, 0], total[:, 1])
    leaving[...] = jnp.where(first, total[:, 1], total[:, 0])


def split_gradient(core, left, right, groups):
    count, width = left.shape
    columns = right.shape[1]
    tile = 256
    rows = width // (2 * groups)
    out = pl.BlockSpec((groups, rows, tile), lambda j, core: (0, 0, j))
    return pl.pallas_call(
        split_kernel,
        grid_spec=pltpu.PrefetchScalarGridSpec(
            num_scalar_prefetch=1,
            grid=(columns // tile,),
            in_specs=[
                pl.BlockSpec((count, width), lambda j, core: (0, 0), pipeline_mode=pl.Buffered(1)),
                pl.BlockSpec((count, tile), lambda j, core: (0, j)),
            ],
            out_specs=[out, out],
        ),
        out_shape=[jax.ShapeDtypeStruct((groups, rows, columns), BF16)] * 2,
        compiler_params=pltpu.CompilerParams(vmem_limit_bytes=40 * 2**20),
        cost_estimate=pl.CostEstimate(
            flops=2 * count * width * columns,
            bytes_accessed=2 * (count * (width + columns) + width * columns),
            transcendentals=0,
        ),
        name="split_gradient",
    )(core.reshape(1).astype(jnp.int32), left, right)


def per_device(
    tokens,
    lengths,
    permutation,
    cotangent,
    norm1_gain,
    mixer_in,
    mixer_gate,
    conv_kernel,
    mixer_out,
    norm2_gain,
    ffn_gate,
    ffn_up,
    ffn_down,
):
    micro, length, width = tokens.shape
    count_b, count_z = lax.axis_size("b"), lax.axis_size("z")
    ia, ib, ic, iz = (lax.axis_index(n) for n in EVERY)
    place = ((ia * count_b + ib) * 2 + ic) * count_z + iz
    per_block = BLOCK // length
    blocks = permutation.shape[1]
    local = conv_kernel.shape[1]
    rows = micro * length

    dealt = lax.dynamic_slice_in_dim(permutation, place // per_block, 1, axis=1)[:, 0]
    own = dealt * per_block + place % per_block
    spots = jnp.arange(blocks, dtype=jnp.int32)

    def holder(piece):
        at = jnp.sum(jnp.where(permutation == (piece // per_block)[:, None], spots[None, :], 0), axis=1)
        return at * per_block + piece % per_block

    before = holder(jnp.maximum(own - 1, 0))
    last = blocks * per_block - 1
    behind = holder(jnp.minimum(own + 1, last))
    order = jnp.arange(lengths.shape[1], dtype=jnp.int32)
    offsets = jnp.sum(jnp.where(order[None, None, :] < order[None, :, None], lengths[:, None, :], 0), axis=2)
    position = own[:, None] * length + jnp.arange(length, dtype=jnp.int32)[None, :]
    is_start = jnp.any(position[:, :, None] == offsets[:, None, :], axis=2)
    was_start = jnp.any(position[:, :, None] - 1 == offsets[:, None, :], axis=2)
    keep_one = jnp.where(is_start, 0.0, 1.0).astype(F32)[:, :, None]
    keep_two = jnp.where(is_start | was_start, 0.0, 1.0).astype(F32)[:, :, None]

    units = -(-ffn_gate.shape[1] // 128) * 128
    spare = ((0, 0), (0, units - ffn_gate.shape[1]))

    def rows_of(pieces):
        return lax.all_gather(jnp.concatenate(pieces, axis=1), ("a", "b", "c"), axis=0, tiled=True)

    def told_at_once(value):
        return lax.all_gather(lax.all_gather(value, "z", axis=0), ("a", "b", "c"), axis=0)

    def in_plane(value):
        value = value.reshape(2, count_b, *value.shape[1:])
        mine = lax.dynamic_index_in_dim(value, ic, 0, keepdims=False)
        far = shift_by(lax.dynamic_index_in_dim(value, 1 - ic, 0, keepdims=False), "c", 1)
        value = in_order([mine, far], "c", 1)
        pieces = [lax.dynamic_index_in_dim(value, ib, 0, keepdims=False)]
        for s in range(1, count_b):
            leaving = lax.dynamic_index_in_dim(value, (ib + s) % count_b, 0, keepdims=False)
            pieces.append(shift_by(leaving, "b", s))
        return pieces

    def plane_rows(pieces):
        value = in_order(pieces, "b", 0)
        return value.reshape(-1, *value.shape[2:])

    bits = exchange_order()
    told_rows = tokens[:, length - 2 :, :].reshape(1, micro * 2, width)
    pad_g, pad_u, pad_d = (jnp.pad(w, spare) for w in (ffn_gate, ffn_up, ffn_down))
    z_in = pieces_of(mixer_in, "z")
    z_bits = [b for b in bits if b < count_z]
    told_rows = told(told_rows, z_bits)
    taps = told(conv_kernel[None], z_bits)
    far_cotangent = pieces_of(cotangent.reshape(rows, width), "b")
    before_at = [entry_of(before[m] ^ place) for m in range(micro)]
    behind_at = [(behind[m] // count_z, behind[m] % count_z) for m in range(micro)]
    z_in, told_rows, taps, far_cotangent, mixer_gate, mixer_out, pad_g, before_at, behind_at = phase(
        z_in, told_rows, taps, far_cotangent, mixer_gate, mixer_out, pad_g, before_at, behind_at
    )
    w_in = rows_of(z_in)
    z_gate = pieces_of(mixer_gate, "z")
    near_g = near_pieces(pad_g, "z")
    z_gate, near_g, told_rows, mixer_out, pad_u, pad_d = phase(z_gate, near_g, told_rows, mixer_out, pad_u, pad_d)
    w_gate = rows_of(z_gate)
    z_out = pieces_of(mixer_out, "z")
    z_g = far_pieces(pad_g, near_g, "z")
    told_rows = told(told_rows, bits[len(z_bits) : -2])
    z_out, z_g, told_rows, pad_u, pad_d, w_in = phase(z_out, z_g, told_rows, pad_u, pad_d, w_in)
    w_out = rows_of(z_out)
    plane_g = in_plane(in_order(z_g, "z", 0))
    z_u = pieces_of(pad_u, "z")
    told_rows = told(told_rows, bits[-2:])
    plane_g, z_u, told_rows, pad_d, w_gate = phase(plane_g, z_u, told_rows, pad_d, w_gate)
    y_g = pieces_of(plane_rows(plane_g), "a")
    plane_u = in_plane(in_order(z_u, "z", 0))
    z_d = pieces_of(pad_d, "z")
    kernel = jnp.concatenate(
        [
            lax.dynamic_index_in_dim(taps, iz ^ ((iz - s) % count_z), 0, keepdims=False)
            for s in range(count_z)
        ],
        axis=1,
    )
    rows_u, half_d = plane_rows(plane_u), in_order(z_d, "z", 0)
    y_g, rows_u, half_d, w_out = phase(y_g, rows_u, half_d, w_out)
    y_u = pieces_of(rows_u, "a")
    plane_d = in_plane(half_d)
    ffn_g = in_order(y_g, "a", 0).reshape(-1, units)

    tail_in = jnp.concatenate(
        [
            lax.dynamic_slice(told_rows, (before_at[m], 2 * m, 0), (1, 2, width))[0]
            for m in range(micro)
        ]
    ).astype(F32)
    local_in = tokens.reshape(rows, width).astype(F32)
    local_cot = cotangent.reshape(rows, width).astype(F32)
    scale_one = lax.rsqrt(jnp.mean(local_in * local_in, axis=1, keepdims=True) + EPSILON)
    normed_one = local_in * scale_one
    hidden_one = (normed_one * norm1_gain).astype(BF16)
    tail_scale = lax.rsqrt(jnp.mean(tail_in * tail_in, axis=1, keepdims=True) + EPSILON)
    tail_hidden = (tail_in * tail_scale * norm1_gain).astype(BF16)
    channels = kernel.shape[1]
    signal = dot_nn(hidden_one, w_in).reshape(micro, length, channels)
    tail_signal = dot_nn(tail_hidden, w_in).reshape(micro, 2, channels)
    gating = dot_nn(hidden_one, w_gate).reshape(micro, length, channels)
    extended = jnp.concatenate([tail_signal, signal], axis=1)
    shift_one = keep_one * extended[:, 1 : length + 1, :]
    shift_two = keep_two * extended[:, 0:length, :]
    mixed = kernel[0] * signal + kernel[1] * shift_one + kernel[2] * shift_two
    product = (mixed * gating).astype(BF16).reshape(rows, channels)
    residual = local_in + dot_nt(product, w_out)

    scale_two = lax.rsqrt(jnp.mean(residual * residual, axis=1, keepdims=True) + EPSILON)
    normed_two = residual * scale_two
    hidden_own = (normed_two * norm2_gain).astype(BF16)


    def with_core(pieces):
        return [v for piece in pieces for v in (piece, shift_by(piece, "c", 1))]

    plane_d, y_u, ffn_g, hidden_own = phase(plane_d, y_u, ffn_g, hidden_own)
    y_d = pieces_of(plane_rows(plane_d), "a")
    ffn_u = in_order(y_u, "a", 0).reshape(-1, units)
    far_hidden = pieces_of(hidden_own, "b")[1:]
    hidden_parts = with_core([hidden_own])
    kept = feed_forward(False, 0, count_b, hidden_parts, (), (ffn_g, ffn_u), ())
    y_d, far_hidden, kept = phase(y_d, far_hidden, kept)
    hidden_parts = hidden_parts + with_core(far_hidden)
    for s in range(1, count_b):
        kept = feed_forward(False, s, count_b, hidden_parts[2 * s : 2 * s + 2], (), (ffn_g, ffn_u), kept)
    gates, ups, activated = kept
    ffn_d = in_order(y_d, "a", 0).reshape(-1, units)
    cot_parts = with_core(far_cotangent)
    other = 1 - ia
    leaving_down = gradient_half(other, cot_parts, activated, units)
    leaving_down, cot_parts, hidden_parts = phase(leaving_down, cot_parts, hidden_parts)
    come_down = shift_by(leaving_down, "a", 1)
    held, backs, outs = (), [None] * count_b, [None] * count_b
    for s in reversed(range(count_b)):
        pair = cot_parts[2 * s : 2 * s + 2]
        *held, near_back, far_back, near_out, far_out = feed_forward(
            True, s, count_b, pair, (gates, ups, activated), (ffn_g, ffn_u, ffn_d), held
        )
        backs[s] = (near_back, shift_by(far_back, "c", 1))
        outs[s] = (near_out, shift_by(far_out, "c", 1))
    grads = held[0]

    def to_owners(sums):
        return [(near.astype(F32) + far.astype(F32)).astype(BF16) for near, far in sums]

    def passed(values):
        return [shift_by(v, "b", -1 - i) for i, v in enumerate(values)]

    def over_z(stay, come):
        return lax.psum_scatter(joined([stay, come]).astype(BF16), "z", scatter_dimension=0, tiled=True)

    leaving_gate = gradient_half(other, hidden_parts, grads, units)
    own_back, own_out = backs[0], outs[0]
    leaving_gate, come_down, far_backs, far_outs, hidden_parts, cot_parts = phase(
        leaving_gate, come_down, backs[1:], outs[1:], hidden_parts, cot_parts
    )
    come_gate, came_back = shift_by(leaving_gate, "a", 1), passed(to_owners(far_backs))
    leaving_up = gradient_half(other, hidden_parts, grads, units, 1)
    stay_down = gradient_half(ia, cot_parts, activated, units)
    stay_gate = gradient_half(ia, hidden_parts, grads, units)
    stay_up = gradient_half(ia, hidden_parts, grads, units, 1)
    leaving_out = to_owners(far_outs)
    scattered_down = over_z(stay_down, come_down)
    come_gate, came_back, leaving_up, stay_gate, stay_up, own_back, own_out, leaving_out = phase(
        come_gate, came_back, leaving_up, stay_gate, stay_up, own_back, own_out, leaving_out
    )
    come_up, came_out = shift_by(leaving_up, "a", 1), passed(leaving_out)
    scattered_gate = over_z(stay_gate, come_gate)
    grad_hidden_two = joined([*own_back, *came_back])

    grad_gain_two = jnp.sum(grad_hidden_two * normed_two, axis=0)
    grad_norm_two = grad_hidden_two * norm2_gain
    inner_two = jnp.mean(grad_norm_two * normed_two, axis=1, keepdims=True)
    grad_residual = local_cot + scale_two * (grad_norm_two - normed_two * inner_two)
    grad_branch = grad_residual.astype(BF16)
    grad_product = dot_nn(grad_branch, w_out).reshape(micro, length, channels)
    def over_c(split):
        kept, leaving = split
        shape = (2, count_b, *kept.shape[1:])
        return [kept.reshape(shape), shift_by(leaving, "c", 1).reshape(shape)]

    def split(left, right):
        return split_gradient(ic, left, right, 2 * count_b)

    out_split = split(grad_branch, product)
    grad_mixed = grad_product * gating
    grad_gating = (grad_product * mixed).astype(BF16).reshape(rows, channels)
    grad_kernel = jnp.stack(
        [
            jnp.sum(grad_mixed * signal, axis=(0, 1)),
            jnp.sum(grad_mixed * shift_one, axis=(0, 1)),
            jnp.sum(grad_mixed * shift_two, axis=(0, 1)),
        ]
    )
    into_one = kernel[1] * (keep_one * grad_mixed)
    into_two = kernel[2] * (keep_two * grad_mixed)
    leaving = jnp.stack([into_two[:, 0], into_one[:, 0] + into_two[:, 1]], axis=1)
    blocked = leaving.reshape(micro, 2, count_z, local)

    def turned(value, dim):
        picks = [
            lax.dynamic_index_in_dim(value, (iz - j) % count_z, dim, keepdims=False) for j in range(count_z)
        ]
        return jnp.concatenate(picks, axis=-1)

    blocked = turned(blocked, 2).reshape(micro * 2, channels).astype(BF16)
    gate_split = split(hidden_one, grad_gating)
    from_gating = dot_nt(grad_gating, w_gate)
    blocked, come_up, came_out, out_split, gate_split, grad_mixed, from_gating, scattered_down = phase(
        blocked, come_up, came_out, out_split, gate_split, grad_mixed, from_gating, scattered_down
    )
    everyone = told_at_once(blocked)
    out_c, gate_c = over_c(out_split), over_c(gate_split)
    everyone, out_c, gate_c, grad_mixed, scattered_gate, scattered_down, come_up = phase(
        everyone, out_c, gate_c, grad_mixed, scattered_gate, scattered_down, come_up
    )
    scattered_up = over_z(stay_up, come_up)
    out_b = parted(out_c, "b", 1)
    gate_a = parted(gate_c, "a", 0)
    down_home = home(scattered_down)
    into_one = kernel[1] * (keep_one * grad_mixed)
    into_two = kernel[2] * (keep_two * grad_mixed)
    arrived = jnp.stack(
        [
            lax.dynamic_slice(
                everyone, (*behind_at[m], 2 * m, 0), (1, 1, 2, channels)
            )[0, 0]
            for m in range(micro)
        ]
    )
    arrived = turned(arrived.reshape(micro, 2, count_z, local), 2).astype(F32)
    arrived = jnp.where((own == last)[:, None, None], 0.0, arrived)
    from_one = jnp.concatenate([into_one[:, 1:], arrived[:, 1:]], axis=1)
    from_two = jnp.concatenate([into_two[:, 2:], arrived[:, :1], jnp.zeros_like(arrived[:, :1])], axis=1)
    grad_signal = (kernel[0] * grad_mixed + from_one + from_two).astype(BF16).reshape(rows, channels)
    in_split = split(hidden_one, grad_signal)
    grad_hidden_one = dot_nt(grad_signal, w_in) + from_gating
    grad_gain_one = jnp.sum(grad_hidden_one * normed_one, axis=0)
    grad_norm_one = grad_hidden_one * norm1_gain
    inner_one = jnp.mean(grad_norm_one * normed_one, axis=1, keepdims=True)
    input_grad = grad_residual + scale_one * (grad_norm_one - normed_one * inner_one)
    out_b, gate_a, in_split, input_grad, down_home, scattered_gate, grad_gain_one, own_out = phase(
        out_b, gate_a, in_split, input_grad, down_home, scattered_gate, grad_gain_one, own_out
    )
    in_c = over_c(in_split)
    middle = channels // 128 * 5 // 7 * 128
    in_a = parted([t[..., :middle] for t in in_c], "a", 0)
    in_b = parted([t[..., middle:] for t in in_c], "b", 1)
    gate_b = parted(settled(gate_a, "a", 0), "b", 0)
    out_a = parted(settled(out_b, "b", 1), "a", 0)
    gate_home, up_home = home(scattered_gate), home(scattered_up)
    by_place = (2, count_b, 2, count_z, -1)
    both_gains = jnp.stack([g.reshape(by_place) for g in (grad_gain_one, grad_gain_two)], axis=3)
    kernel_parts = turned(grad_kernel.reshape(3, count_z, local), 1).reshape(3, count_z, 2, count_b, 2, -1)
    small = jnp.concatenate([both_gains, kernel_parts.transpose(2, 3, 4, 0, 1, 5)], axis=3)
    small = parted([small], "c", 2, F32)
    in_a, in_b, gate_b, out_a, gate_home, up_home, down_home, own_out, small = phase(
        in_a, in_b, gate_b, out_a, gate_home, up_home, down_home, own_out, small
    )
    small = parted(settled(small, "c", 2), "a", 0, F32)
    small = parted(settled(small, "a", 0), "b", 0, F32)
    in_a, in_b = parted(settled(in_a, "a", 0), "b", 0), parted(settled(in_b, "b", 1), "a", 0)
    two_z = columns_home([jnp.concatenate([joined(settled(out_a, "a", 0)), joined(settled(gate_b, "b", 0))], axis=0)])
    in_a, in_b, two_z, small, own_out = phase(in_a, in_b, two_z, small, own_out)
    output = (joined([*own_out, *came_out]) + residual).astype(BF16)
    small = joined(settled(small, "b", 0))
    share = small.shape[2]
    small = turned(jnp.pad(small, ((0, 3), (0, 0), (0, local - share))), 1)
    in_rows = jnp.concatenate([joined(settled(in_a, "b", 0)), joined(settled(in_b, "a", 0))], axis=1)
    in_z = columns_home([jnp.concatenate([in_rows, small], axis=0)])
    grad_out, grad_gate_w = jnp.split(joined(two_z), 2)
    in_z = joined(in_z)
    grad_in_w, small = in_z[: in_rows.shape[0]], in_z[in_rows.shape[0] :, :share]
    hidden_units = ffn_gate.shape[1]
    grad_ffg, grad_ffu, grad_down = (g[:, :hidden_units].astype(F32) for g in (gate_home, up_home, down_home))

    return (
        output.reshape(micro, length, width),
        input_grad.reshape(micro, length, width),
        small[0],
        grad_in_w,
        grad_gate_w,
        small[2:5],
        grad_out,
        small[1],
        grad_ffg,
        grad_ffu,
        grad_down,
    )


def solution(mesh):
    row, col = mesh.shape["row"], mesh.shape["col"]
    fine = Mesh(mesh.devices.reshape(2, row // 4, 2, col), EVERY)
    by_rows = ("a", "b", "c")
    matrix = P(by_rows, "z")
    token = P(None, EVERY, None)
    return jax.shard_map(
        per_device,
        mesh=fine,
        in_specs=(
            token,
            P(),
            P(),
            token,
            P(),
            matrix,
            matrix,
            P(None, "z"),
            matrix,
            P(),
            matrix,
            matrix,
            matrix,
        ),
        out_specs=(
            token,
            token,
            P(EVERY),
            matrix,
            matrix,
            P(None, ("z", *by_rows)),
            matrix,
            P(EVERY),
            matrix,
            matrix,
            matrix,
        ),
        check_vma=False,
    )
```
